32 devices in a mesh: groups: 2 (over x), grid: 4 (over y, core), depth: 4 (over z).
Axes of the slice: x: 2, y: 2, z: 4, core: 2. Of those that a mesh axis runs over, the one named last changes fastest.
Arguments:
- patch_rows: bfloat16 [2048, 6144], P(('groups', 'depth'), 'grid'), parts along dimension 0, may hold values from -6 to 6
- qkv_blocks: bfloat16 [4, 3072, 3, 12, 128], P('grid'), may hold values from -0.078125 to 0.078125
- out_blocks: bfloat16 [4, 1536, 3072], P('grid'), may hold values from -0.109375 to 0.109375
- out_grad: bfloat16 [2048, 6144], P(('groups', 'depth'), 'grid'), parts along dimension 0, may hold values from -6 to 6
Outputs:
- attention_out: bfloat16 [2048, 6144], P(('groups', 'depth'), 'grid'), parts along dimension 0
- input_grad: bfloat16 [2048, 6144], P(('groups', 'depth'), 'grid'), parts along dimension 0
- qkv_grad: bfloat16 [8, 3072, 3, 12, 128], P(('groups', 'grid'), 'depth'), parts along dimension 0
- out_proj_grad: bfloat16 [8, 1536, 3072], P(('groups', 'grid'), 'depth'), parts along dimension 0
The draws below stay inside these ranges and needn't reach their ends.
There are 2 independent parts, one for each index of `groups`. The reference program is written for one: setup_inputs(seed, part) draws one part's arguments, and reference() takes and returns one part's arrays. A program takes and returns all parts, laid end to end along the dimension named above; an argument that names none is the same for every part. Nothing has to cross between parts.
All inputs are finite; a program needn't handle non-finite values.
Results may differ from the reference program's by a relative error of at most 0.022.
Values may be sent and summed in bfloat16 or wider, within the bound.
No kernel may reach another device: no remote copies, remote signals or barrier semaphores. Data moves between devices by JAX's collectives and lax.ppermute only.
A program may use at most 256 MiB of HBM per device.

```python
import jax
import jax.numpy as jnp
from jax import lax

D = 6144
H = 24
HD = 128
PATCHES = 256
GRIDS = 4
Q = 2
DQ = 3072
HQ = 12
SLICE_ROWS = 256
IMAGES = 4
ROWS = 1024
N_DEPTH = 4


def block_levels(stream_key, extent, shards, low, top_value):
    gain, own = 1.0, jax.random.fold_in(stream_key, 6)
    for dim, shards_of in shards:
        steps = jnp.exp(jax.random.uniform(jax.random.fold_in(own, dim), (shards_of,), jnp.float32, low / len(shards), top_value / len(shards)))
        gain = gain * jnp.repeat(steps, extent[dim] // shards_of).reshape([-1 if axis == dim else 1 for axis in range(len(extent))])
    return gain


def noise(own_key, dims, scale, reach, pieces=(), kind=jnp.bfloat16):
    values = scale * jax.random.normal(own_key, dims, jnp.float32)
    if pieces:
        values = values * block_levels(own_key, dims, pieces, -0.22, 0.18)
    return jnp.clip(values, -reach, reach).astype(kind)


def setup_inputs(seed: int = 0, part: int = 0) -> dict:
    arg_keys = jax.random.split(jax.random.key(seed), 5)
    own_keys = jax.random.split(jax.random.fold_in(arg_keys[4], part), 5)
    patch_rows = noise(own_keys[0], (ROWS, D), 1.0, 6.0, ((0, 4), (1, 4)))
    qkv_blocks = noise(arg_keys[1], (GRIDS, DQ, 3, HQ, HD), D ** -0.5, 0.078125, ((0, 4),))
    out_blocks = noise(arg_keys[2], (GRIDS, HQ * HD, DQ), (H * HD) ** -0.5, 0.109375, ((0, 4),))
    out_grad = noise(own_keys[3], (ROWS, D), 1.0, 6.0, ((0, 4), (1, 4)))
    return dict(patch_rows=patch_rows, qkv_blocks=qkv_blocks, out_blocks=out_blocks, out_grad=out_grad)


eps = 1e-06

def normalize(vectors):
    center = vectors - lax.optimization_barrier(jnp.mean(vectors, axis=-1, keepdims=True))
    spread = lax.optimization_barrier(jnp.mean(center * center, axis=-1, keepdims=True))
    sigma = jnp.sqrt(spread + eps)
    return (center / sigma, sigma)

def normalize_back(grads, normed, sigma):
    first_mean = lax.optimization_barrier(jnp.mean(grads, axis=-1, keepdims=True))
    second_mean = lax.optimization_barrier(jnp.mean(grads * normed, axis=-1, keepdims=True))
    return (grads - first_mean - normed * second_mean) / sigma

def reference(patch_rows, qkv_blocks, out_blocks, out_grad):
    width = H * HD
    scale = HD ** (-0.5)
    qkv_full = qkv_blocks.reshape(Q, Q, DQ, 3, HQ, HD).transpose(0, 2, 3, 1, 4, 5).reshape(D, 3 * width)
    out_full = out_blocks.reshape(Q, Q, HQ * HD, DQ).transpose(1, 2, 0, 3).reshape(width, D)
    proj = jnp.dot(patch_rows, qkv_full, preferred_element_type=jnp.float32).reshape(ROWS, 3, H, HD)
    q_hat, q_sigma = normalize(proj[:, 0])
    k_hat, k_sigma = normalize(proj[:, 1])
    queries = q_hat.astype(jnp.bfloat16)
    keys = k_hat.astype(jnp.bfloat16)
    values = proj[:, 2].astype(jnp.bfloat16)
    d_attended = jnp.dot(out_grad, out_full.T, preferred_element_type=jnp.float32).astype(jnp.bfloat16)
    d_attended = d_attended.reshape(ROWS, H, HD)

    def per_image(items):
        q_img, k_img, v_img, qh_img, qs_img, kh_img, ks_img, do_img = items
        qf = q_img.astype(jnp.float32)
        kf = k_img.astype(jnp.float32)
        vf = v_img.astype(jnp.float32)
        dof = do_img.astype(jnp.float32)
        scores = jnp.einsum('qhe,khe->hqk', qf, kf) * scale
        expo = jnp.exp(scores)
        probs = expo / lax.optimization_barrier(jnp.sum(expo, axis=-1, keepdims=True))
        probs_low = probs.astype(jnp.bfloat16)
        attended = jnp.einsum('hqk,khe->qhe', probs_low.astype(jnp.float32), vf).astype(jnp.bfloat16)
        d_probs = jnp.einsum('qhe,khe->hqk', dof, vf)
        d_values = jnp.einsum('hqk,qhe->khe', probs_low.astype(jnp.float32), dof)
        d_scores = (probs * (d_probs - lax.optimization_barrier(jnp.sum(probs * d_probs, axis=-1, keepdims=True)))).astype(jnp.bfloat16)
        d_queries = jnp.einsum('hqk,khe->qhe', d_scores.astype(jnp.float32), kf) * scale
        d_keys = jnp.einsum('hqk,qhe->khe', d_scores.astype(jnp.float32), qf) * scale
        dq_raw = normalize_back(d_queries, qh_img, qs_img)
        dk_raw = normalize_back(d_keys, kh_img, ks_img)
        d_proj = jnp.stack([dq_raw, dk_raw, d_values], axis=1).astype(jnp.bfloat16)
        return (attended, d_proj)

    def by_image(array):
        return array.reshape((IMAGES, PATCHES) + array.shape[1:])
    attended, d_proj = lax.map(per_image, (by_image(queries), by_image(keys), by_image(values), by_image(q_hat), by_image(q_sigma), by_image(k_hat), by_image(k_sigma), by_image(d_attended)))
    attended = attended.reshape(ROWS, width)
    d_proj = d_proj.reshape(ROWS, 3 * width)
    attention_out = jnp.dot(attended, out_full, preferred_element_type=jnp.float32).astype(jnp.bfloat16)
    input_grad = jnp.dot(d_proj, qkv_full.T, preferred_element_type=jnp.float32).astype(jnp.bfloat16)
    grad_in = jnp.zeros((D, 3 * width), jnp.float32)
    grad_out = jnp.zeros((width, D), jnp.float32)
    for depth_index in range(N_DEPTH):
        lower = depth_index * SLICE_ROWS
        upper = lower + SLICE_ROWS
        term_in = jnp.dot(patch_rows[lower:upper].T, d_proj[lower:upper], preferred_element_type=jnp.float32).astype(jnp.bfloat16)
        term_out = jnp.dot(attended[lower:upper].T, out_grad[lower:upper], preferred_element_type=jnp.float32).astype(jnp.bfloat16)
        term_in = lax.optimization_barrier(term_in)
        term_out = lax.optimization_barrier(term_out)
        grad_in = grad_in + term_in.astype(jnp.float32)
        grad_out = grad_out + term_out.astype(jnp.float32)
    qkv_grad = grad_in.astype(jnp.bfloat16).reshape(Q, DQ, 3, Q, HQ, HD).transpose(0, 3, 1, 2, 4, 5).reshape(GRIDS, DQ, 3, HQ, HD)
    out_proj_grad = grad_out.astype(jnp.bfloat16).reshape(Q, HQ * HD, Q, DQ).transpose(2, 0, 1, 3).reshape(GRIDS, HQ * HD, DQ)
    return (attention_out, input_grad, qkv_grad, out_proj_grad)
```

```python
import functools
import math

import jax
import jax.numpy as jnp
from jax import lax
from jax.experimental import pallas as pl
from jax.experimental.pallas import tpu as pltpu
from jax.sharding import PartitionSpec as P

PATCHES = 256


eps = 1e-06


def partner_2(value, axis, stride):
    mask = 2**stride
    pairs = [(source, source ^ mask) for source in range(lax.axis_size(axis))]
    return lax.ppermute(value, axis, pairs)


def normalize(vectors):
    center = vectors - jnp.mean(vectors, axis=-1, keepdims=True)
    spread = jnp.mean(center * center, axis=-1, keepdims=True)
    sigma = jnp.sqrt(spread + eps)
    return (center / sigma, sigma)


def normalize_back(grads, normed, sigma):
    first_mean = jnp.mean(grads, axis=-1, keepdims=True)
    second_mean = jnp.mean(grads * normed, axis=-1, keepdims=True)
    return (grads - first_mean - normed * second_mean) / sigma


def collect_panel(pieces, first_bit, count, position, along):
    for section in range(count):
        partner = partner_2(pieces, "grid", first_bit + section)
        higher = position >> section & 1
        pieces = jnp.where(
            higher == 1,
            jnp.concatenate([partner, pieces], along),
            jnp.concatenate([pieces, partner], along),
        )
    return pieces


def reduce_panel(partial_sum, first_bit, count, position, along):
    for section in reversed(range(count)):
        half_size = partial_sum.shape[along] // 2
        higher = position >> section & 1
        kept = lax.dynamic_slice_in_dim(partial_sum, higher * half_size, half_size, along)
        outgoing = lax.dynamic_slice_in_dim(partial_sum, (1 - higher) * half_size, half_size, along)
        partial_sum = kept + partner_2(
            outgoing.astype(jnp.bfloat16), "grid", first_bit + section
        ).astype(outgoing.dtype)
    return partial_sum


def contract(left, right, left_dim, right_dim):
    return lax.dot_general(
        left, right, (((left_dim,), (right_dim,)), ((), ())), preferred_element_type=jnp.float32
    )


def local(patch_rows, qkv_blocks, out_blocks, out_grad):
    side = math.isqrt(lax.axis_size("grid"))
    bit_count = side.bit_length() - 1
    grid_index = lax.axis_index("grid")
    row_place = grid_index // side
    col_place = grid_index % side
    slice_rows = patch_rows.shape[0]
    block_width = qkv_blocks.shape[1]
    heads_local = qkv_blocks.shape[3]
    head_dim = qkv_blocks.shape[4]
    width_local = heads_local * head_dim
    query_rows = slice_rows // side
    scale = head_dim ** (-0.5)
    x_panel = collect_panel(patch_rows, 0, bit_count, col_place, 1)
    w_in = qkv_blocks[0].reshape(block_width, 3 * width_local)
    partial_proj = jnp.dot(x_panel, w_in, preferred_element_type=jnp.float32)
    proj_local = reduce_panel(partial_proj, bit_count, bit_count, row_place, 0)
    proj_local = proj_local.reshape(query_rows, 3, heads_local, head_dim)
    query_raw = proj_local[:, 0]
    k_hat, k_sigma = normalize(proj_local[:, 1])
    kv_local = jnp.stack(
        [k_hat.astype(jnp.bfloat16), proj_local[:, 2].astype(jnp.bfloat16)], axis=1
    )
    kv_gathered = collect_panel(kv_local, bit_count, bit_count, row_place, 0)
    keys_all = kv_gathered[:, 0]
    values_all = kv_gathered[:, 1]
    q_hat, q_sigma = normalize(query_raw)
    queries = q_hat.astype(jnp.bfloat16)
    group_count = max(1, query_rows // PATCHES)
    key_rows = max(query_rows, PATCHES)
    group_shape = (group_count, key_rows // group_count, heads_local, head_dim)
    keys = keys_all.reshape(group_shape)
    values = values_all.reshape(group_shape)
    query_group = queries.reshape(group_count, query_rows // group_count, heads_local, head_dim)
    scores = (
        jnp.einsum("gqhe,gkhe->ghqk", query_group, keys, preferred_element_type=jnp.float32) * scale
    )
    expo = jnp.exp(scores)
    probs = expo / jnp.sum(expo, axis=-1, keepdims=True)
    probs_low = probs.astype(jnp.bfloat16)
    attended = jnp.einsum("ghqk,gkhe->gqhe", probs_low, values, preferred_element_type=jnp.float32)
    attended = attended.astype(jnp.bfloat16).reshape(query_rows, width_local)
    attended_panel = collect_panel(attended, bit_count, bit_count, row_place, 0)
    w_back = out_blocks[0]
    out_partial = jnp.dot(attended_panel, w_back, preferred_element_type=jnp.float32)
    attention_out = reduce_panel(out_partial, 0, bit_count, col_place, 1).astype(jnp.bfloat16)
    grad_panel = collect_panel(out_grad, 0, bit_count, col_place, 1)
    d_att_partial = contract(grad_panel, w_back, 1, 1)
    d_attended = reduce_panel(d_att_partial, bit_count, bit_count, row_place, 0).astype(
        jnp.bfloat16
    )
    d_attended = d_attended.reshape(group_count, query_rows // group_count, heads_local, head_dim)
    grad_out_part = contract(attended_panel, grad_panel, 0, 0)
    d_probs = jnp.einsum("gqhe,gkhe->ghqk", d_attended, values, preferred_element_type=jnp.float32)
    d_values = jnp.einsum(
        "ghqk,gqhe->gkhe", probs_low, d_attended, preferred_element_type=jnp.float32
    )
    d_scores = (probs * (d_probs - jnp.sum(probs * d_probs, axis=-1, keepdims=True))).astype(
        jnp.bfloat16
    )
    d_queries = (
        jnp.einsum("ghqk,gkhe->gqhe", d_scores, keys, preferred_element_type=jnp.float32) * scale
    )
    d_keys = (
        jnp.einsum("ghqk,gqhe->gkhe", d_scores, query_group, preferred_element_type=jnp.float32)
        * scale
    )
    key_terms = jnp.stack(
        [
            d_keys.reshape(key_rows, heads_local, head_dim),
            d_values.reshape(key_rows, heads_local, head_dim),
        ],
        axis=1,
    )
    key_sums = reduce_panel(key_terms, bit_count, bit_count, row_place, 0)
    dq_raw = normalize_back(d_queries.reshape(query_rows, heads_local, head_dim), q_hat, q_sigma)
    dk_raw = normalize_back(key_sums[:, 0], k_hat, k_sigma)
    d_proj = (
        jnp.stack([dq_raw, dk_raw, key_sums[:, 1]], axis=1)
        .astype(jnp.bfloat16)
        .reshape(query_rows, 3 * width_local)
    )
    d_proj_panel = collect_panel(d_proj, bit_count, bit_count, row_place, 0)
    input_partial = contract(d_proj_panel, w_in, 1, 1)
    input_grad = reduce_panel(input_partial, 0, bit_count, col_place, 1).astype(jnp.bfloat16)
    grad_in_part = contract(x_panel, d_proj_panel, 0, 0)
    grad_in, grad_out = (
        lax.psum_scatter(
            grad_in_part.astype(jnp.bfloat16), "depth", scatter_dimension=0, tiled=True
        ).astype(jnp.float32),
        lax.psum_scatter(
            grad_out_part.astype(jnp.bfloat16), "depth", scatter_dimension=0, tiled=True
        ).astype(jnp.float32),
    )
    qkv_grad = grad_in.astype(jnp.bfloat16).reshape(1, grad_in.shape[0], 3, heads_local, head_dim)
    out_proj_grad = grad_out.astype(jnp.bfloat16)[None]
    return (attention_out, input_grad, qkv_grad, out_proj_grad)


def y_swap(value):
    return partner_2(value, "grid", 1)


def core_swap(value):
    return partner_2(value, "grid", 0)


def params(*semantics):
    return pltpu.CompilerParams(dimension_semantics=semantics, vmem_limit_bytes=56 * 2**20)


def proj_kernel(place_ref, own_ref, other_ref, w_own_ref, w_other_ref, keep_ref, send_ref):
    heads = w_own_ref.shape[1]
    columns = [(part, head) for head in range(heads) for part in range(3)]
    w_own = jnp.concatenate([w_own_ref[part, head] for part, head in columns], axis=1)
    total = jnp.dot(own_ref[...], w_own, preferred_element_type=jnp.float32)
    w_other = jnp.concatenate([w_other_ref[part, head] for part, head in columns], axis=1)
    total += jnp.dot(other_ref[...], w_other, preferred_element_type=jnp.float32)

    @pl.when(pl.program_id(0) == 0)
    def _():
        send_ref[...] = total.astype(send_ref.dtype)

    @pl.when(pl.program_id(0) == 1)
    def _():
        keep_ref[...] = total


def project(place, x_own, x_other, weights, start, heads):
    rows, piece = x_own.shape
    head_dim = weights.shape[3]
    per_half = weights.shape[1] // 2 // heads
    width = heads * 3 * head_dim

    def head_block(step, place):
        return (place[0] + 1 + step) % 2 * per_half + start // heads

    whole = pl.BlockSpec((rows, piece), lambda step, place: (0, 0))
    block = (3, heads, piece, head_dim)
    result = pl.BlockSpec((rows, width), lambda step, place: (0, 0))
    return pl.pallas_call(
        proj_kernel,
        grid_spec=pltpu.PrefetchScalarGridSpec(
            num_scalar_prefetch=1,
            grid=(2,),
            in_specs=[
                whole,
                whole,
                pl.BlockSpec(block, lambda step, place: (0, head_block(step, place), place[1], 0)),
                pl.BlockSpec(
                    block, lambda step, place: (0, head_block(step, place), 1 - place[1], 0)
                ),
            ],
            out_specs=[result, result],
        ),
        out_shape=[
            jax.ShapeDtypeStruct((rows, width), jnp.float32),
            jax.ShapeDtypeStruct((rows, width), jnp.bfloat16),
        ],
        compiler_params=params("arbitrary"),
        cost_estimate=pl.CostEstimate(
            flops=8 * rows * piece * width,
            bytes_accessed=8 * piece * width + 4 * rows * piece + 6 * rows * width,
            transcendentals=0,
        ),
        name="project",
    )(place, x_own, x_other, weights, weights)


def attention_kernel(scale, keep_ref, recv_ref, d_out_ref, att_ref, d_proj_ref):
    head_dim = d_out_ref.shape[1]
    low = jnp.bfloat16

    def part(index):
        columns = slice(index * head_dim, (index + 1) * head_dim)
        return keep_ref[:, columns] + recv_ref[:, columns].astype(jnp.float32)

    def dot(left, right, left_dim, right_dim):
        return contract(left, right, left_dim, right_dim)

    q_hat, q_sigma = normalize(part(0))
    k_hat, k_sigma = normalize(part(1))
    queries, keys, values = q_hat.astype(low), k_hat.astype(low), part(2).astype(low)
    d_out = d_out_ref[...]
    expo = jnp.exp(dot(queries, keys, 1, 1) * scale)
    probs = expo / jnp.sum(expo, axis=-1, keepdims=True)
    probs_low = probs.astype(low)
    att_ref[...] = dot(probs_low, values, 1, 0).astype(low)
    d_probs = dot(d_out, values, 1, 1)
    d_values = dot(probs_low, d_out, 0, 0)
    weighted = probs * d_probs
    d_scores = (weighted - probs * jnp.sum(weighted, axis=-1, keepdims=True)).astype(low)
    d_queries = dot(d_scores, keys, 1, 0) * scale
    d_keys = dot(d_scores, queries, 0, 0) * scale
    d_proj_ref[:, :head_dim] = normalize_back(d_queries, q_hat, q_sigma).astype(low)
    d_proj_ref[:, head_dim : 2 * head_dim] = normalize_back(d_keys, k_hat, k_sigma).astype(low)
    d_proj_ref[:, 2 * head_dim :] = d_values.astype(low)


def attend(keep, recv, d_attended, start, heads, head_dim):
    rows = keep.shape[0]
    triple = pl.BlockSpec((rows, 3 * head_dim), lambda head: (0, head))
    single = pl.BlockSpec((rows, head_dim), lambda head: (0, head))
    return pl.pallas_call(
        functools.partial(attention_kernel, head_dim ** (-0.5)),
        grid=(heads,),
        in_specs=[triple, triple, pl.BlockSpec((rows, head_dim), lambda head: (0, start + head))],
        out_specs=[single, triple],
        out_shape=[
            jax.ShapeDtypeStruct((rows, heads * head_dim), jnp.bfloat16),
            jax.ShapeDtypeStruct((rows, heads * 3 * head_dim), jnp.bfloat16),
        ],
        compiler_params=params("arbitrary"),
        cost_estimate=pl.CostEstimate(
            flops=14 * heads * rows * rows * head_dim,
            bytes_accessed=28 * heads * rows * head_dim,
            transcendentals=heads * rows * rows,
        ),
        name="attend",
    )(keep, recv, d_attended)


def input_kernel(first, last, place_ref, d_own_ref, d_other_ref, w_own_ref, w_other_ref, *refs):
    acc_own_ref, acc_other_ref = refs[-2:]
    step = pl.program_id(0)
    heads = w_own_ref.shape[1]
    columns = [(part, head) for head in range(heads) for part in range(3)]

    def add(grads):
        for w_ref, acc_ref in ((w_own_ref, acc_own_ref), (w_other_ref, acc_other_ref)):
            w = jnp.concatenate([w_ref[part, head] for part, head in columns], axis=1)
            acc_ref[...] += contract(grads, w, 1, 1)

    @pl.when(step == 0)
    def _():
        if first:
            acc_own_ref[...] = jnp.zeros_like(acc_own_ref)
            acc_other_ref[...] = jnp.zeros_like(acc_other_ref)
        else:
            acc_own_ref[...] = refs[0][...]
            acc_other_ref[...] = refs[1][...]
        add(d_own_ref[...])

    @pl.when(step == 1)
    def _():
        add(d_other_ref[...])
        if last:
            refs[-4][...] = acc_own_ref[...]
            refs[-3][...] = acc_other_ref[...].astype(refs[-3].dtype)
        else:
            refs[-4][...] = acc_own_ref[...]
            refs[-3][...] = acc_other_ref[...]


def input_terms(place, d_own, d_other, weights, start, heads, sums, last):
    rows = d_own.shape[0]
    head_dim = weights.shape[3]
    piece = weights.shape[2] // 2
    per_half = weights.shape[1] // 2 // heads
    width = heads * 3 * head_dim

    def head_block(step, place):
        return (place[0] + step) % 2 * per_half + start // heads

    block = (3, heads, piece, head_dim)
    total = pl.BlockSpec((rows, piece), lambda step, place: (0, 0))
    sums = () if sums is None else tuple(sums)
    return pl.pallas_call(
        functools.partial(input_kernel, not sums, last),
        grid_spec=pltpu.PrefetchScalarGridSpec(
            num_scalar_prefetch=1,
            grid=(2,),
            in_specs=[
                pl.BlockSpec((rows, width), lambda step, place: (0, 0)),
                pl.BlockSpec((rows, width), lambda step, place: (place[2], 0)),
                pl.BlockSpec(block, lambda step, place: (0, head_block(step, place), place[1], 0)),
                pl.BlockSpec(
                    block, lambda step, place: (0, head_block(step, place), 1 - place[1], 0)
                ),
            ]
            + [total] * len(sums),
            out_specs=[total, total],
            scratch_shapes=[pltpu.VMEM((rows, piece), jnp.float32)] * 2,
        ),
        out_shape=[
            jax.ShapeDtypeStruct((rows, piece), jnp.float32),
            jax.ShapeDtypeStruct((rows, piece), jnp.bfloat16 if last else jnp.float32),
        ],
        compiler_params=params("arbitrary"),
        cost_estimate=pl.CostEstimate(
            flops=8 * rows * piece * width,
            bytes_accessed=8 * piece * width + 16 * rows * piece,
            transcendentals=0,
        ),
        name="input_terms",
    )(place, d_own, d_other, weights, weights, *sums)


def weight_kernel(depth, place_ref, x_ref, d_own_ref, d_other_ref, *refs):
    out_ref = refs[-1]
    heads, head_dim = out_ref.shape[1], out_ref.shape[3]
    patches = x_ref.shape[1] // depth

    def fill(grads_ref):
        total = None
        for slot in range(depth):
            image = lax.rem(place_ref[2] + slot, depth)
            rows = pl.ds(pl.multiple_of(image * patches, patches), patches)
            term = jnp.dot(
                x_ref[:, slot * patches : (slot + 1) * patches],
                grads_ref[rows, :],
                preferred_element_type=jnp.float32,
            )
            total = term if total is None else total + term
        for head in range(heads):
            for part in range(3):
                column = (head * 3 + part) * head_dim
                out_ref[part, head] = total[:, column : column + head_dim].astype(out_ref.dtype)

    @pl.when(pl.program_id(0) == 0)
    def _():
        fill(d_own_ref)

    @pl.when(pl.program_id(0) == 1)
    def _():
        fill(d_other_ref)


def weight_terms(place, depth, x_slots, d_own, d_other, start, heads, shape, filled):
    rows, width = d_own.shape
    block_rows = x_slots.shape[0]
    head_dim = shape[3]
    per_half = shape[1] // 2 // heads
    whole = pl.BlockSpec((rows, width), lambda step, place: (0, 0))
    filled = () if filled is None else (filled,)
    return pl.pallas_call(
        functools.partial(weight_kernel, depth),
        grid_spec=pltpu.PrefetchScalarGridSpec(
            num_scalar_prefetch=1,
            grid=(2,),
            in_specs=[
                pl.BlockSpec((block_rows, rows), lambda step, place: (0, 0)),
                whole,
                whole,
            ]
            + [pl.BlockSpec(memory_space=pl.ANY)] * len(filled),
            out_specs=pl.BlockSpec(
                (3, heads, block_rows, head_dim),
                lambda step, place: (0, (place[0] + step) % 2 * per_half + start // heads, 0, 0),
            ),
        ),
        out_shape=jax.ShapeDtypeStruct(shape, jnp.bfloat16),
        input_output_aliases={4: 0} if filled else {},
        compiler_params=params("arbitrary"),
        cost_estimate=pl.CostEstimate(
            flops=4 * rows * block_rows * width,
            bytes_accessed=2 * rows * block_rows + 4 * rows * width + 4 * block_rows * width,
            transcendentals=0,
        ),
        name="weight_terms",
    )(place, x_slots, d_own, d_other, *filled)


def ordered(place, own, other, along):
    return jnp.where(
        place == 0,
        jnp.concatenate([own, other], along),
        jnp.concatenate([other, own], along),
    )


def line_gather(value, axis):
    count = lax.axis_size(axis)
    place = lax.axis_index(axis)
    upper, lower = [value], [value]
    for step in range(1, count):
        upper.append(lax.ppermute(upper[-1], axis, [(d + 1, d) for d in range(count - step)]))
        lower.append(lax.ppermute(lower[-1], axis, [(d - 1, d) for d in range(step, count)]))
    return [value] + [
        jnp.where(place + slot < count, upper[slot], lower[count - slot])
        for slot in range(1, count)
    ]


def send_slots(blocks_of, axis):
    count = lax.axis_size(axis)
    place = lax.axis_index(axis)
    slots = [blocks_of(place)]
    for slot in range(1, count):
        target = (place + count - slot) % count
        pairs = [(d, (d + count - slot) % count) for d in range(count)]
        slots.append(lax.ppermute(blocks_of(target), axis, pairs))
    return slots


def local_heads(patch_rows, qkv_blocks, out_blocks, out_grad):
    depth = lax.axis_size("depth")
    grid_index = lax.axis_index("grid")
    row_place, col_place = grid_index // 2, grid_index % 2
    depth_place = lax.axis_index("depth")
    place = jnp.stack([row_place, col_place, depth_place]).astype(jnp.int32)
    rows, piece = patch_rows.shape
    heads_local, head_dim = qkv_blocks.shape[3:]
    heads_half = heads_local // 2
    half = heads_half * head_dim
    weights = qkv_blocks[0].transpose(1, 2, 0, 3)
    w_back = out_blocks[0]
    low = jnp.bfloat16
    sizes = [2, 2, 1, 1] if heads_half == 6 else [1] * heads_half
    chunks = [(sum(sizes[:index]), size) for index, size in enumerate(sizes)]

    x_other = core_swap(patch_rows)
    g_other = core_swap(out_grad)
    projected = []
    for start, heads in chunks:
        keep, send = project(place, patch_rows, x_other, weights, start, heads)
        projected.append((keep, y_swap(send)))
    grad_panel = ordered(col_place, out_grad, g_other, 1)
    d_att_partial = contract(grad_panel, w_back, 1, 1)
    d_att_send = lax.dynamic_slice_in_dim(d_att_partial, (1 - row_place) * half, half, 1)
    d_att_keep = lax.dynamic_slice_in_dim(d_att_partial, row_place * half, half, 1)
    d_attended = (d_att_keep + y_swap(d_att_send.astype(low)).astype(jnp.float32)).astype(low)

    x_panel = ordered(col_place, patch_rows, x_other, 1)
    block_rows = x_panel.shape[1] // depth
    part_rows = block_rows // 2
    x_parts = send_slots(
        lambda target: lax.dynamic_slice_in_dim(
            x_panel, target * block_rows + col_place * part_rows, part_rows, 1
        ),
        "depth",
    )
    x_part = jnp.concatenate(x_parts, axis=0).T
    x_slots = ordered(col_place, x_part, core_swap(x_part), 0)

    g_own = jnp.concatenate(line_gather(out_grad, "depth"), axis=0)
    g_slots = ordered(col_place, g_own, core_swap(g_own), 1)

    shape = (3, heads_local, block_rows, head_dim)
    attended_own, attended_other, gathered = [], [], []
    for (start, heads), (keep, recv) in zip(chunks, projected):
        attended, d_proj = attend(keep, recv, d_attended, start, heads, head_dim)
        attended_own.append(attended)
        attended_other.append(y_swap(attended))
        d_own = lax.all_gather(d_proj, "depth", axis=0, tiled=True)
        gathered.append((d_proj, d_own, y_swap(d_own)))
    attended_panel = ordered(
        row_place,
        jnp.concatenate(attended_own, axis=1),
        jnp.concatenate(attended_other, axis=1),
        1,
    )
    out_partial = jnp.dot(attended_panel, w_back, preferred_element_type=jnp.float32)
    attention_out = reduce_panel(out_partial, 0, 1, col_place, 1).astype(low)
    grad_rows = w_back.shape[0] // depth
    a_slots = jnp.concatenate(
        send_slots(
            lambda target: lax.dynamic_slice_in_dim(
                attended_panel, target * grad_rows, grad_rows, 1
            ),
            "depth",
        ),
        axis=0,
    )
    out_proj_grad = contract(a_slots, g_slots, 0, 0).astype(low)

    sums, filled = None, None
    for index, ((start, heads), (d_proj, d_own, d_other)) in enumerate(zip(chunks, gathered)):
        last = index == len(chunks) - 1
        sums = input_terms(place, d_proj, d_other, weights, start, heads, sums, last)
        filled = weight_terms(
            place, depth, x_slots, d_own, d_other, start, heads, shape, filled
        )
    input_grad = (sums[0] + core_swap(sums[1]).astype(jnp.float32)).astype(low)
    qkv_grad = filled.transpose(2, 0, 1, 3)[None]
    return (attention_out, input_grad, qkv_grad, out_proj_grad[None])


def local_any(patch_rows, qkv_blocks, out_blocks, out_grad):
    by_heads = (
        lax.axis_size("grid") == 4
        and qkv_blocks.shape[3] % 2 == 0
        and patch_rows.shape[0] == PATCHES
        and qkv_blocks.shape[1] % (2 * lax.axis_size("depth")) == 0
        and out_blocks.shape[1] % lax.axis_size("depth") == 0
        and lax.axis_size("depth") <= 4
    )
    body = local_heads if by_heads else local
    return body(patch_rows, qkv_blocks, out_blocks, out_grad)


def solution(mesh):
    return jax.shard_map(
        local_any,
        mesh=mesh,
        in_specs=(
            P(("groups", "depth"), "grid"),
            P("grid", None, None, None, None),
            P("grid", None, None),
            P(("groups", "depth"), "grid"),
        ),
        out_specs=(
            P(("groups", "depth"), "grid"),
            P(("groups", "depth"), "grid"),
            P(("groups", "grid"), "depth", None, None, None),
            P(("groups", "grid"), "depth", None),
        ),
        check_vma=False,
    )
```

```python
import functools
import math

import jax
import jax.numpy as jnp
from jax import lax
from jax.experimental import pallas as pl
from jax.experimental.pallas import tpu as pltpu
from jax.sharding import PartitionSpec as P

PATCHES = 256


eps = 1e-06


def partner_2(value, axis, stride):
    mask = 2**stride
    pairs = [(source, source ^ mask) for source in range(lax.axis_size(axis))]
    return lax.ppermute(value, axis, pairs)


def normalize(vectors):
    center = vectors - jnp.mean(vectors, axis=-1, keepdims=True)
    spread = jnp.mean(center * center, axis=-1, keepdims=True)
    sigma = jnp.sqrt(spread + eps)
    return (center / sigma, sigma)


def normalize_back(grads, normed, sigma):
    first_mean = jnp.mean(grads, axis=-1, keepdims=True)
    second_mean = jnp.mean(grads * normed, axis=-1, keepdims=True)
    return (grads - first_mean - normed * second_mean) / sigma


def collect_panel(pieces, first_bit, count, position, along):
    for section in range(count):
        partner = partner_2(pieces, "grid", first_bit + section)
        higher = position >> section & 1
        pieces = jnp.where(
            higher == 1,
            jnp.concatenate([partner, pieces], along),
            jnp.concatenate([pieces, partner], along),
        )
    return pieces


def reduce_panel(partial_sum, first_bit, count, position, along):
    for section in reversed(range(count)):
        half_size = partial_sum.shape[along] // 2
        higher = position >> section & 1
        kept = lax.dynamic_slice_in_dim(partial_sum, higher * half_size, half_size, along)
        outgoing = lax.dynamic_slice_in_dim(partial_sum, (1 - higher) * half_size, half_size, along)
        partial_sum = kept + partner_2(
            outgoing.astype(jnp.bfloat16), "grid", first_bit + section
        ).astype(outgoing.dtype)
    return partial_sum


def contract(left, right, left_dim, right_dim):
    return lax.dot_general(
        left, right, (((left_dim,), (right_dim,)), ((), ())), preferred_element_type=jnp.float32
    )


def local(patch_rows, qkv_blocks, out_blocks, out_grad):
    side = math.isqrt(lax.axis_size("grid"))
    bit_count = side.bit_length() - 1
    grid_index = lax.axis_index("grid")
    row_place = grid_index // side
    col_place = grid_index % side
    slice_rows = patch_rows.shape[0]
    block_width = qkv_blocks.shape[1]
    heads_local = qkv_blocks.shape[3]
    head_dim = qkv_blocks.shape[4]
    width_local = heads_local * head_dim
    query_rows = slice_rows // side
    scale = head_dim ** (-0.5)
    x_panel = collect_panel(patch_rows, 0, bit_count, col_place, 1)
    w_in = qkv_blocks[0].reshape(block_width, 3 * width_local)
    partial_proj = jnp.dot(x_panel, w_in, preferred_element_type=jnp.float32)
    proj_local = reduce_panel(partial_proj, bit_count, bit_count, row_place, 0)
    proj_local = proj_local.reshape(query_rows, 3, heads_local, head_dim)
    query_raw = proj_local[:, 0]
    k_hat, k_sigma = normalize(proj_local[:, 1])
    kv_local = jnp.stack(
        [k_hat.astype(jnp.bfloat16), proj_local[:, 2].astype(jnp.bfloat16)], axis=1
    )
    kv_gathered = collect_panel(kv_local, bit_count, bit_count, row_place, 0)
    keys_all = kv_gathered[:, 0]
    values_all = kv_gathered[:, 1]
    q_hat, q_sigma = normalize(query_raw)
    queries = q_hat.astype(jnp.bfloat16)
    group_count = max(1, query_rows // PATCHES)
    key_rows = max(query_rows, PATCHES)
    group_shape = (group_count, key_rows // group_count, heads_local, head_dim)
    keys = keys_all.reshape(group_shape)
    values = values_all.reshape(group_shape)
    query_group = queries.reshape(group_count, query_rows // group_count, heads_local, head_dim)
    scores = (
        jnp.einsum("gqhe,gkhe->ghqk", query_group, keys, preferred_element_type=jnp.float32) * scale
    )
    expo = jnp.exp(scores)
    probs = expo / jnp.sum(expo, axis=-1, keepdims=True)
    probs_low = probs.astype(jnp.bfloat16)
    attended = jnp.einsum("ghqk,gkhe->gqhe", probs_low, values, preferred_element_type=jnp.float32)
    attended = attended.astype(jnp.bfloat16).reshape(query_rows, width_local)
    attended_panel = collect_panel(attended, bit_count, bit_count, row_place, 0)
    w_back = out_blocks[0]
    out_partial = jnp.dot(attended_panel, w_back, preferred_element_type=jnp.float32)
    attention_out = reduce_panel(out_partial, 0, bit_count, col_place, 1).astype(jnp.bfloat16)
    grad_panel = collect_panel(out_grad, 0, bit_count, col_place, 1)
    d_att_partial = contract(grad_panel, w_back, 1, 1)
    d_attended = reduce_panel(d_att_partial, bit_count, bit_count, row_place, 0).astype(
        jnp.bfloat16
    )
    d_attended = d_attended.reshape(group_count, query_rows // group_count, heads_local, head_dim)
    grad_out_part = contract(attended_panel, grad_panel, 0, 0)
    d_probs = jnp.einsum("gqhe,gkhe->ghqk", d_attended, values, preferred_element_type=jnp.float32)
    d_values = jnp.einsum(
        "ghqk,gqhe->gkhe", probs_low, d_attended, preferred_element_type=jnp.float32
    )
    d_scores = (probs * (d_probs - jnp.sum(probs * d_probs, axis=-1, keepdims=True))).astype(
        jnp.bfloat16
    )
    d_queries = (
        jnp.einsum("ghqk,gkhe->gqhe", d_scores, keys, preferred_element_type=jnp.float32) * scale
    )
    d_keys = (
        jnp.einsum("ghqk,gqhe->gkhe", d_scores, query_group, preferred_element_type=jnp.float32)
        * scale
    )
    key_terms = jnp.stack(
        [
            d_keys.reshape(key_rows, heads_local, head_dim),
            d_values.reshape(key_rows, heads_local, head_dim),
        ],
        axis=1,
    )
    key_sums = reduce_panel(key_terms, bit_count, bit_count, row_place, 0)
    dq_raw = normalize_back(d_queries.reshape(query_rows, heads_local, head_dim), q_hat, q_sigma)
    dk_raw = normalize_back(key_sums[:, 0], k_hat, k_sigma)
    d_proj = (
        jnp.stack([dq_raw, dk_raw, key_sums[:, 1]], axis=1)
        .astype(jnp.bfloat16)
        .reshape(query_rows, 3 * width_local)
    )
    d_proj_panel = collect_panel(d_proj, bit_count, bit_count, row_place, 0)
    input_partial = contract(d_proj_panel, w_in, 1, 1)
    input_grad = reduce_panel(input_partial, 0, bit_count, col_place, 1).astype(jnp.bfloat16)
    grad_in_part = contract(x_panel, d_proj_panel, 0, 0)
    grad_in, grad_out = (
        lax.psum_scatter(
            grad_in_part.astype(jnp.bfloat16), "depth", scatter_dimension=0, tiled=True
        ).astype(jnp.float32),
        lax.psum_scatter(
            grad_out_part.astype(jnp.bfloat16), "depth", scatter_dimension=0, tiled=True
        ).astype(jnp.float32),
    )
    qkv_grad = grad_in.astype(jnp.bfloat16).reshape(1, grad_in.shape[0], 3, heads_local, head_dim)
    out_proj_grad = grad_out.astype(jnp.bfloat16)[None]
    return (attention_out, input_grad, qkv_grad, out_proj_grad)


SIZES = [6]
HINT = 4096


def y_swap(value):
    return partner_2(value, "grid", 1)


def core_swap(value):
    return partner_2(value, "grid", 0)


def hint(flops, bytes_accessed, transcendentals):
    return pl.CostEstimate(
        flops=flops // HINT, bytes_accessed=bytes_accessed // HINT, transcendentals=transcendentals
    )


def params(*semantics):
    return pltpu.CompilerParams(dimension_semantics=semantics, vmem_limit_bytes=56 * 2**20)


def proj_kernel(place_ref, own_ref, other_ref, w_own_ref, w_other_ref, out_ref):
    heads = w_own_ref.shape[1]
    columns = [(part, head) for head in range(heads) for part in range(3)]
    w_own = jnp.concatenate([w_own_ref[part, head] for part, head in columns], axis=1)
    total = jnp.dot(own_ref[...], w_own, preferred_element_type=jnp.float32)
    w_other = jnp.concatenate([w_other_ref[part, head] for part, head in columns], axis=1)
    total += jnp.dot(other_ref[...], w_other, preferred_element_type=jnp.float32)
    out_ref[...] = total.astype(out_ref.dtype)


def project(place, x_own, x_other, weights, swap, start, heads, kind):
    rows, piece = x_own.shape
    head_dim = weights.shape[3]
    group = 2 if heads % 2 == 0 and start % 2 == 0 else 1
    if start % 3 == 0 and heads % 3 == 0:
        group = 3
    per_half = weights.shape[1] // 2 // group
    width = heads * 3 * head_dim

    def head_block(step, place):
        return (place[0] + swap) % 2 * per_half + start // group + step

    whole = pl.BlockSpec((rows, piece), lambda step, place: (0, 0))
    block = (3, group, piece, head_dim)
    return pl.pallas_call(
        proj_kernel,
        grid_spec=pltpu.PrefetchScalarGridSpec(
            num_scalar_prefetch=1,
            grid=(heads // group,),
            in_specs=[
                whole,
                whole,
                pl.BlockSpec(block, lambda step, place: (0, head_block(step, place), place[1], 0)),
                pl.BlockSpec(
                    block, lambda step, place: (0, head_block(step, place), 1 - place[1], 0)
                ),
            ],
            out_specs=pl.BlockSpec((rows, group * 3 * head_dim), lambda step, place: (0, step)),
        ),
        out_shape=jax.ShapeDtypeStruct((rows, width), kind),
        compiler_params=params("arbitrary"),
        cost_estimate=hint(
            flops=4 * rows * piece * width,
            bytes_accessed=4 * piece * width + 4 * rows * piece + 4 * rows * width,
            transcendentals=0,
        ),
        name="project",
    )(place, x_own, x_other, weights, weights)


def attention_kernel(scale, keep_ref, recv_ref, d_out_ref, att_ref, d_proj_ref):
    head_dim = d_out_ref.shape[1]
    low = jnp.bfloat16

    def part(index):
        columns = slice(index * head_dim, (index + 1) * head_dim)
        return keep_ref[:, columns] + recv_ref[:, columns].astype(jnp.float32)

    def dot(left, right, left_dim, right_dim):
        return contract(left, right, left_dim, right_dim)

    q_hat, q_sigma = normalize(part(0))
    k_hat, k_sigma = normalize(part(1))
    queries, keys, values = q_hat.astype(low), k_hat.astype(low), part(2).astype(low)
    d_out = d_out_ref[...]
    expo = jnp.exp(dot(queries, keys, 1, 1) * scale)
    probs = expo / jnp.sum(expo, axis=-1, keepdims=True)
    probs_low = probs.astype(low)
    att_ref[...] = dot(probs_low, values, 1, 0).astype(low)
    d_probs = dot(d_out, values, 1, 1)
    d_values = dot(probs_low, d_out, 0, 0)
    weighted = probs * d_probs
    d_scores = (weighted - probs * jnp.sum(weighted, axis=-1, keepdims=True)).astype(low)
    d_queries = dot(d_scores, keys, 1, 0) * scale
    d_keys = dot(d_scores, queries, 0, 0) * scale
    d_proj_ref[:, :head_dim] = normalize_back(d_queries, q_hat, q_sigma).astype(low)
    d_proj_ref[:, head_dim : 2 * head_dim] = normalize_back(d_keys, k_hat, k_sigma).astype(low)
    d_proj_ref[:, 2 * head_dim :] = d_values.astype(low)


def attend(keep, recv, d_attended, start, heads, head_dim):
    rows = keep.shape[0]
    triple = pl.BlockSpec((rows, 3 * head_dim), lambda head: (0, head))
    single = pl.BlockSpec((rows, head_dim), lambda head: (0, head))
    return pl.pallas_call(
        functools.partial(attention_kernel, head_dim ** (-0.5)),
        grid=(heads,),
        in_specs=[triple, triple, pl.BlockSpec((rows, head_dim), lambda head: (0, start + head))],
        out_specs=[single, triple],
        out_shape=[
            jax.ShapeDtypeStruct((rows, heads * head_dim), jnp.bfloat16),
            jax.ShapeDtypeStruct((rows, heads * 3 * head_dim), jnp.bfloat16),
        ],
        compiler_params=params("arbitrary"),
        cost_estimate=hint(
            flops=14 * heads * rows * rows * head_dim,
            bytes_accessed=28 * heads * rows * head_dim,
            transcendentals=0,
        ),
        name="attend",
    )(keep, recv, d_attended)


def input_kernel(place_ref, d_own_ref, d_other_ref, w_own_ref, w_other_ref, *refs):
    keep_ref, send_ref, acc_own_ref, acc_other_ref = refs
    step, steps = pl.program_id(0), pl.num_programs(0)
    heads = w_own_ref.shape[1]
    columns = [(part, head) for head in range(heads) for part in range(3)]

    @pl.when(step == 0)
    def _():
        acc_own_ref[...] = jnp.zeros_like(acc_own_ref)
        acc_other_ref[...] = jnp.zeros_like(acc_other_ref)

    def add(grads):
        for w_ref, acc_ref in ((w_own_ref, acc_own_ref), (w_other_ref, acc_other_ref)):
            w = jnp.concatenate([w_ref[part, head] for part, head in columns], axis=1)
            acc_ref[...] += contract(w, grads, 1, 1)

    @pl.when(step < steps // 2)
    def _():
        add(d_own_ref[...])

    @pl.when(step >= steps // 2)
    def _():
        add(d_other_ref[...])

    @pl.when(step == steps - 1)
    def _():
        keep_ref[...] = acc_own_ref[...].T
        send_ref[...] = acc_other_ref[...].T.astype(send_ref.dtype)


def input_terms(place, d_own, d_other, weights):
    rows, width = d_own.shape
    head_dim = weights.shape[3]
    piece = weights.shape[2] // 2
    heads_half = weights.shape[1] // 2
    group = 2 if heads_half % 2 == 0 else 1
    steps = heads_half // group

    def head_block(step, place):
        return (place[0] + step // steps) % 2 * steps + step % steps

    block = (3, group, piece, head_dim)
    total = pl.BlockSpec((rows, piece), lambda step, place: (0, 0))
    grads = (rows, group * 3 * head_dim)
    return pl.pallas_call(
        input_kernel,
        grid_spec=pltpu.PrefetchScalarGridSpec(
            num_scalar_prefetch=1,
            grid=(2 * steps,),
            in_specs=[
                pl.BlockSpec(grads, lambda step, place: (0, jnp.minimum(step, steps - 1))),
                pl.BlockSpec(grads, lambda step, place: (0, jnp.maximum(step - steps, 0))),
                pl.BlockSpec(block, lambda step, place: (0, head_block(step, place), place[1], 0)),
                pl.BlockSpec(
                    block, lambda step, place: (0, head_block(step, place), 1 - place[1], 0)
                ),
            ],
            out_specs=[total, total],
            scratch_shapes=[pltpu.VMEM((piece, rows), jnp.float32)] * 2,
        ),
        out_shape=[
            jax.ShapeDtypeStruct((rows, piece), jnp.float32),
            jax.ShapeDtypeStruct((rows, piece), jnp.bfloat16),
        ],
        compiler_params=params("arbitrary"),
        cost_estimate=hint(
            flops=8 * rows * piece * width,
            bytes_accessed=8 * piece * width + 10 * rows * piece,
            transcendentals=0,
        ),
        name="input_terms",
    )(place, d_own, d_other, weights, weights)


def weight_kernel(count, place_ref, x_ref, *refs):
    slots, out_ref, x_sorted = refs[:count], refs[-2], refs[-1]
    heads, head_dim = out_ref.shape[1], out_ref.shape[3]
    patches = x_ref.shape[0] // count

    @pl.when(pl.program_id(0) == 0)
    def _():
        for slot in range(count):
            offset = pl.multiple_of(place_ref[2 + slot] * patches, patches)
            x_sorted[:, slot * patches : (slot + 1) * patches] = x_ref[pl.ds(offset, patches), :].T

    grads = jnp.concatenate([slot_ref[...] for slot_ref in slots], axis=0)
    total = jnp.dot(x_sorted[...], grads, preferred_element_type=jnp.float32)
    for head in range(heads):
        for part in range(3):
            column = (head * 3 + part) * head_dim
            out_ref[part, head] = total[:, column : column + head_dim].astype(out_ref.dtype)


def weight_terms(place, x_slots, slots, swap, start, shape, filled):
    count = len(slots)
    rows, width = slots[0].shape
    block_rows = x_slots.shape[1]
    head_dim = shape[3]
    heads = width // (3 * head_dim)
    group = 2 if heads % 2 == 0 and start % 2 == 0 else 1
    per_half = shape[1] // 2 // group
    part = pl.BlockSpec((rows, group * 3 * head_dim), lambda step, place: (0, step))
    filled = () if filled is None else (filled,)
    return pl.pallas_call(
        functools.partial(weight_kernel, count),
        grid_spec=pltpu.PrefetchScalarGridSpec(
            num_scalar_prefetch=1,
            grid=(heads // group,),
            in_specs=[pl.BlockSpec(x_slots.shape, lambda step, place: (0, 0))]
            + [part] * count
            + [pl.BlockSpec(memory_space=pl.ANY)] * len(filled),
            out_specs=pl.BlockSpec(
                (3, group, block_rows, head_dim),
                lambda step, place: (
                    0,
                    (place[0] + swap) % 2 * per_half + start // group + step,
                    0,
                    0,
                ),
            ),
            scratch_shapes=[pltpu.VMEM(x_slots.shape[::-1], x_slots.dtype)],
        ),
        out_shape=jax.ShapeDtypeStruct(shape, jnp.bfloat16),
        input_output_aliases={2 + count: 0} if filled else {},
        compiler_params=params("arbitrary"),
        cost_estimate=hint(
            flops=2 * count * rows * block_rows * width,
            bytes_accessed=2 * count * rows * (block_rows + width) + 2 * block_rows * width,
            transcendentals=0,
        ),
        name="weight_terms",
    )(place, x_slots, *slots, *filled)


def out_kernel(count, place_ref, att_ref, *refs):
    own, other, out_ref, att_turned = refs[:count], refs[count : 2 * count], refs[-2], refs[-1]

    @pl.when(pl.program_id(0) == 0)
    def _():
        att_turned[...] = att_ref[...].T

    def fill(slots):
        grads = jnp.concatenate([slot_ref[...] for slot_ref in slots], axis=0)
        total = jnp.dot(att_turned[...], grads, preferred_element_type=jnp.float32)
        out_ref[...] = total.astype(out_ref.dtype)

    half = pl.num_programs(0) // 2

    @pl.when(pl.program_id(0) < half)
    def _():
        fill(own)

    @pl.when(pl.program_id(0) >= half)
    def _():
        fill(other)


def out_terms(place, att_slots, own, other):
    count = len(own)
    width = own[0].shape[1]
    steps = 2 if width % 256 == 0 else 1
    block = width // steps
    rows, block_rows = att_slots.shape
    return pl.pallas_call(
        functools.partial(out_kernel, count),
        grid_spec=pltpu.PrefetchScalarGridSpec(
            num_scalar_prefetch=1,
            grid=(2 * steps,),
            in_specs=[pl.BlockSpec((rows, block_rows), lambda step, place: (0, 0))]
            + [
                pl.BlockSpec(
                    (slot.shape[0], block),
                    lambda step, place: (0, jnp.minimum(step, steps - 1)),
                )
                for slot in own
            ]
            + [
                pl.BlockSpec(
                    (slot.shape[0], block),
                    lambda step, place: (0, jnp.maximum(step - steps, 0)),
                )
                for slot in other
            ],
            out_specs=pl.BlockSpec(
                (block_rows, block),
                lambda step, place: (
                    0,
                    (place[1] + step // steps) % 2 * steps + step % steps,
                ),
            ),
            scratch_shapes=[pltpu.VMEM((block_rows, rows), att_slots.dtype)],
        ),
        out_shape=jax.ShapeDtypeStruct((block_rows, 2 * width), jnp.bfloat16),
        compiler_params=params("arbitrary"),
        cost_estimate=hint(
            flops=4 * rows * block_rows * width,
            bytes_accessed=4 * rows * width + 2 * block_rows * (rows + 2 * width),
            transcendentals=0,
        ),
        name="out_terms",
    )(place, att_slots, *own, *other)


def output_kernel(place_ref, own_ref, other_ref, v_own_ref, v_other_ref, keep_ref, send_ref):
    total = jnp.dot(own_ref[...], v_own_ref[...], preferred_element_type=jnp.float32)
    total += jnp.dot(other_ref[...], v_other_ref[...], preferred_element_type=jnp.float32)

    @pl.when(pl.program_id(0) == 0)
    def _():
        send_ref[...] = total.astype(send_ref.dtype)

    @pl.when(pl.program_id(0) == 1)
    def _():
        keep_ref[...] = total


def output_terms(place, att_own, att_other, w_back):
    rows, half = att_own.shape
    piece = w_back.shape[1] // 2
    whole = pl.BlockSpec((rows, half), lambda step, place: (0, 0))
    result = pl.BlockSpec((rows, piece), lambda step, place: (0, 0))
    return pl.pallas_call(
        output_kernel,
        grid_spec=pltpu.PrefetchScalarGridSpec(
            num_scalar_prefetch=1,
            grid=(2,),
            in_specs=[
                whole,
                whole,
                pl.BlockSpec(
                    (half, piece), lambda step, place: (place[0], (place[1] + 1 + step) % 2)
                ),
                pl.BlockSpec(
                    (half, piece), lambda step, place: (1 - place[0], (place[1] + 1 + step) % 2)
                ),
            ],
            out_specs=[result, result],
        ),
        out_shape=[
            jax.ShapeDtypeStruct((rows, piece), jnp.float32),
            jax.ShapeDtypeStruct((rows, piece), jnp.bfloat16),
        ],
        compiler_params=params("arbitrary"),
        cost_estimate=hint(
            flops=8 * rows * half * piece,
            bytes_accessed=8 * half * piece + 4 * rows * half + 6 * rows * piece,
            transcendentals=0,
        ),
        name="output_terms",
    )(place, att_own, att_other, w_back, w_back)


def ordered(place, own, other, along):
    return jnp.where(
        place == 0,
        jnp.concatenate([own, other], along),
        jnp.concatenate([other, own], along),
    )


def line_step(upper, lower, axis):
    count = lax.axis_size(axis)
    step = len(upper)
    upper.append(lax.ppermute(upper[-1], axis, [(d + 1, d) for d in range(count - step)]))
    lower.append(lax.ppermute(lower[-1], axis, [(d - 1, d) for d in range(step, count)]))


def together(*groups):
    flat, tree = jax.tree.flatten(groups)
    return jax.tree.unflatten(tree, lax.optimization_barrier(flat))


def by_offset(upper, lower, axis):
    count = lax.axis_size(axis)
    place = lax.axis_index(axis)
    return [
        jnp.where(place + slot < count, upper[slot], lower[count - slot])
        for slot in range(1, count)
    ]


def arrivals(count):
    table = []
    for place in range(count):
        found = []
        for step in range(1, count):
            found += [(0, step)] * (place + step < count) + [(1, step)] * (place >= step)
        if place >= count // 2:
            found.sort(key=lambda item: (item[1], -item[0]))
        table.append(found)
    return table


def pick_arrival(upper, lower, index, table, axis):
    place = lax.axis_index(axis)
    picked = None
    for other, found in enumerate(table):
        side, step = found[index]
        source = (upper, lower)[side][step]
        picked = source if picked is None else jnp.where(place == other, source, picked)
    return picked


def send_slots(blocks_of, axis):
    count = lax.axis_size(axis)
    place = lax.axis_index(axis)
    slots = [blocks_of(place)]
    for slot in range(1, count):
        target = (place + count - slot) % count
        pairs = [(d, (d + count - slot) % count) for d in range(count)]
        slots.append(lax.ppermute(blocks_of(target), axis, pairs))
    return slots


def local_heads(patch_rows, qkv_blocks, out_blocks, out_grad):
    depth = lax.axis_size("depth")
    grid_index = lax.axis_index("grid")
    row_place, col_place = grid_index // 2, grid_index % 2
    depth_place = lax.axis_index("depth")
    table = arrivals(depth)
    offsets = [0] + [
        sum(
            jnp.where(depth_place == d, (step if side == 0 else depth - step), 0)
            for d, (side, step) in enumerate(table[d][index] for d in range(depth))
        )
        for index in range(depth - 1)
    ]
    place = jnp.stack([row_place, col_place, *offsets]).astype(jnp.int32)
    heads_local, head_dim = qkv_blocks.shape[3:]
    heads_half = heads_local // 2
    half = heads_half * head_dim
    weights = qkv_blocks[0].transpose(1, 2, 0, 3)
    w_back = out_blocks[0]
    low = jnp.bfloat16
    sizes = SIZES if heads_half == sum(SIZES) else [heads_half]
    chunks = [(sum(sizes[:index]), size) for index, size in enumerate(sizes)]

    x_other = core_swap(patch_rows)
    g_other = core_swap(out_grad)
    received = []
    for start, heads in chunks:
        send = project(place, patch_rows, x_other, weights, 1, start, heads, low)
        received.append(y_swap(send))
    g_line = ([out_grad], [out_grad])
    line_step(*g_line, "depth")
    line_step(*g_line, "depth")
    grad_panel = ordered(col_place, out_grad, g_other, 1)
    d_att_partial = contract(grad_panel, w_back, 1, 1)
    d_att_send = lax.dynamic_slice_in_dim(d_att_partial, (1 - row_place) * half, half, 1)
    d_att_keep = lax.dynamic_slice_in_dim(d_att_partial, row_place * half, half, 1)
    d_attended = (d_att_keep + y_swap(d_att_send.astype(low)).astype(jnp.float32)).astype(low)

    x_panel = ordered(col_place, patch_rows, x_other, 1)
    block_rows = x_panel.shape[1] // depth
    part_rows = block_rows // 2
    x_parts = send_slots(
        lambda target: lax.dynamic_slice_in_dim(
            x_panel, target * block_rows + col_place * part_rows, part_rows, 1
        ),
        "depth",
    )

    shape = (3, heads_local, block_rows, head_dim)
    attended, d_proj = [], []
    for (start, heads), recv in zip(chunks, received):
        keep = project(place, patch_rows, x_other, weights, 0, start, heads, jnp.float32)
        parts = attend(keep, recv, d_attended, start, heads, head_dim)
        attended.append(parts[0])
        d_proj.append(parts[1])
    attended, d_proj = jnp.concatenate(attended, axis=1), jnp.concatenate(d_proj, axis=1)

    d_proj, g_line = together(d_proj, g_line)
    upper, lower = [d_proj], [d_proj]
    own, other = [d_proj], [y_swap(d_proj)]
    attended_other = y_swap(attended)

    line_step(upper, lower, "depth")
    slot = pick_arrival(upper, lower, 0, table, "depth")
    x_part = jnp.concatenate(x_parts, axis=0)
    x_slots = ordered(col_place, x_part, core_swap(x_part), 1)
    upper, lower, slot, other, x_slots, attended_other = together(
        upper, lower, slot, other, x_slots, attended_other
    )
    own.append(slot)
    other.append(y_swap(slot))

    line_step(upper, lower, "depth")
    slot = pick_arrival(upper, lower, 1, table, "depth")
    input_keep, input_send = input_terms(place, own[0], other[0], weights)
    upper, lower, slot, other, input_keep, input_send = together(
        upper, lower, slot, other, input_keep, input_send
    )
    own.append(slot)
    other.append(y_swap(slot))

    line_step(upper, lower, "depth")
    input_grad = (input_keep + core_swap(input_send).astype(jnp.float32)).astype(low)
    slot = pick_arrival(upper, lower, 2, table, "depth")
    attended_panel = ordered(row_place, attended, attended_other, 1)
    out_keep, out_send = output_terms(place, attended, attended_other, w_back)
    slot, x_slots, input_grad, attended_panel, g_line, out_keep, out_send = together(
        slot, x_slots, input_grad, attended_panel, g_line, out_keep, out_send
    )
    own.append(slot)
    other.append(y_swap(slot))

    line_step(*g_line, "depth")
    grad_rows = w_back.shape[0] // depth
    a_slots = send_slots(
        lambda target: lax.dynamic_slice_in_dim(
            attended_panel, target * grad_rows, grad_rows, 1
        ),
        "depth",
    )
    attention_out = (out_keep + core_swap(out_send).astype(jnp.float32)).astype(low)
    filled = weight_terms(place, x_slots, own, 0, 0, shape, None)
    other, g_line, a_slots, attention_out, filled = together(
        other, g_line, a_slots, attention_out, filled
    )

    g_far = jnp.concatenate(by_offset(*g_line, "depth"), axis=0)
    g_far_other = core_swap(g_far)
    filled = weight_terms(place, x_slots, other, 1, 0, shape, filled)
    out_proj_grad = out_terms(
        place,
        jnp.concatenate(a_slots, axis=0),
        [out_grad, g_far],
        [g_other, g_far_other],
    )
    qkv_grad = filled.transpose(2, 0, 1, 3)[None]
    return (attention_out, input_grad, qkv_grad, out_proj_grad[None])


def local_any(patch_rows, qkv_blocks, out_blocks, out_grad):
    by_heads = (
        lax.axis_size("grid") == 4
        and qkv_blocks.shape[3] % 2 == 0
        and patch_rows.shape[0] == PATCHES
        and qkv_blocks.shape[1] % (2 * lax.axis_size("depth")) == 0
        and out_blocks.shape[1] % lax.axis_size("depth") == 0
        and lax.axis_size("depth") == 4
    )
    body = local_heads if by_heads else local
    return body(patch_rows, qkv_blocks, out_blocks, out_grad)


def solution(mesh):
    return jax.shard_map(
        local_any,
        mesh=mesh,
        in_specs=(
            P(("groups", "depth"), "grid"),
            P("grid", None, None, None, None),
            P("grid", None, None),
            P(("groups", "depth"), "grid"),
        ),
        out_specs=(
            P(("groups", "depth"), "grid"),
            P(("groups", "depth"), "grid"),
            P(("groups", "grid"), "depth", None, None, None),
            P(("groups", "grid"), "depth", None),
        ),
        check_vma=False,
    )
```

```python
import functools
import math

import jax
import jax.numpy as jnp
from jax import lax
from jax.experimental import pallas as pl
from jax.experimental.pallas import tpu as pltpu
from jax.sharding import PartitionSpec as P

PATCHES = 256


eps = 1e-06


def partner_2(value, axis, stride):
    mask = 2**stride
    pairs = [(source, source ^ mask) for source in range(lax.axis_size(axis))]
    return lax.ppermute(value, axis, pairs)


def normalize(vectors):
    center = vectors - jnp.mean(vectors, axis=-1, keepdims=True)
    spread = jnp.mean(center * center, axis=-1, keepdims=True)
    sigma = jnp.sqrt(spread + eps)
    return (center / sigma, sigma)


def normalize_back(grads, normed, sigma):
    first_mean = jnp.mean(grads, axis=-1, keepdims=True)
    second_mean = jnp.mean(grads * normed, axis=-1, keepdims=True)
    return (grads - first_mean - normed * second_mean) / sigma


def collect_panel(pieces, first_bit, count, position, along):
    for section in range(count):
        partner = partner_2(pieces, "grid", first_bit + section)
        higher = position >> section & 1
        pieces = jnp.where(
            higher == 1,
            jnp.concatenate([partner, pieces], along),
            jnp.concatenate([pieces, partner], along),
        )
    return pieces


def reduce_panel(partial_sum, first_bit, count, position, along):
    for section in reversed(range(count)):
        half_size = partial_sum.shape[along] // 2
        higher = position >> section & 1
        kept = lax.dynamic_slice_in_dim(partial_sum, higher * half_size, half_size, along)
        outgoing = lax.dynamic_slice_in_dim(partial_sum, (1 - higher) * half_size, half_size, along)
        partial_sum = kept + partner_2(
            outgoing.astype(jnp.bfloat16), "grid", first_bit + section
        ).astype(outgoing.dtype)
    return partial_sum


def contract(left, right, left_dim, right_dim):
    return lax.dot_general(
        left, right, (((left_dim,), (right_dim,)), ((), ())), preferred_element_type=jnp.float32
    )


def local(patch_rows, qkv_blocks, out_blocks, out_grad):
    side = math.isqrt(lax.axis_size("grid"))
    bit_count = side.bit_length() - 1
    grid_index = lax.axis_index("grid")
    row_place = grid_index // side
    col_place = grid_index % side
    slice_rows = patch_rows.shape[0]
    block_width = qkv_blocks.shape[1]
    heads_local = qkv_blocks.shape[3]
    head_dim = qkv_blocks.shape[4]
    width_local = heads_local * head_dim
    query_rows = slice_rows // side
    scale = head_dim ** (-0.5)
    x_panel = collect_panel(patch_rows, 0, bit_count, col_place, 1)
    w_in = qkv_blocks[0].reshape(block_width, 3 * width_local)
    partial_proj = jnp.dot(x_panel, w_in, preferred_element_type=jnp.float32)
    proj_local = reduce_panel(partial_proj, bit_count, bit_count, row_place, 0)
    proj_local = proj_local.reshape(query_rows, 3, heads_local, head_dim)
    query_raw = proj_local[:, 0]
    k_hat, k_sigma = normalize(proj_local[:, 1])
    kv_local = jnp.stack(
        [k_hat.astype(jnp.bfloat16), proj_local[:, 2].astype(jnp.bfloat16)], axis=1
    )
    kv_gathered = collect_panel(kv_local, bit_count, bit_count, row_place, 0)
    keys_all = kv_gathered[:, 0]
    values_all = kv_gathered[:, 1]
    q_hat, q_sigma = normalize(query_raw)
    queries = q_hat.astype(jnp.bfloat16)
    group_count = max(1, query_rows // PATCHES)
    key_rows = max(query_rows, PATCHES)
    group_shape = (group_count, key_rows // group_count, heads_local, head_dim)
    keys = keys_all.reshape(group_shape)
    values = values_all.reshape(group_shape)
    query_group = queries.reshape(group_count, query_rows // group_count, heads_local, head_dim)
    scores = (
        jnp.einsum("gqhe,gkhe->ghqk", query_group, keys, preferred_element_type=jnp.float32) * scale
    )
    expo = jnp.exp(scores)
    probs = expo / jnp.sum(expo, axis=-1, keepdims=True)
    probs_low = probs.astype(jnp.bfloat16)
    attended = jnp.einsum("ghqk,gkhe->gqhe", probs_low, values, preferred_element_type=jnp.float32)
    attended = attended.astype(jnp.bfloat16).reshape(query_rows, width_local)
    attended_panel = collect_panel(attended, bit_count, bit_count, row_place, 0)
    w_back = out_blocks[0]
    out_partial = jnp.dot(attended_panel, w_back, preferred_element_type=jnp.float32)
    attention_out = reduce_panel(out_partial, 0, bit_count, col_place, 1).astype(jnp.bfloat16)
    grad_panel = collect_panel(out_grad, 0, bit_count, col_place, 1)
    d_att_partial = contract(grad_panel, w_back, 1, 1)
    d_attended = reduce_panel(d_att_partial, bit_count, bit_count, row_place, 0).astype(
        jnp.bfloat16
    )
    d_attended = d_attended.reshape(group_count, query_rows // group_count, heads_local, head_dim)
    grad_out_part = contract(attended_panel, grad_panel, 0, 0)
    d_probs = jnp.einsum("gqhe,gkhe->ghqk", d_attended, values, preferred_element_type=jnp.float32)
    d_values = jnp.einsum(
        "ghqk,gqhe->gkhe", probs_low, d_attended, preferred_element_type=jnp.float32
    )
    d_scores = (probs * (d_probs - jnp.sum(probs * d_probs, axis=-1, keepdims=True))).astype(
        jnp.bfloat16
    )
    d_queries = (
        jnp.einsum("ghqk,gkhe->gqhe", d_scores, keys, preferred_element_type=jnp.float32) * scale
    )
    d_keys = (
        jnp.einsum("ghqk,gqhe->gkhe", d_scores, query_group, preferred_element_type=jnp.float32)
        * scale
    )
    key_terms = jnp.stack(
        [
            d_keys.reshape(key_rows, heads_local, head_dim),
            d_values.reshape(key_rows, heads_local, head_dim),
        ],
        axis=1,
    )
    key_sums = reduce_panel(key_terms, bit_count, bit_count, row_place, 0)
    dq_raw = normalize_back(d_queries.reshape(query_rows, heads_local, head_dim), q_hat, q_sigma)
    dk_raw = normalize_back(key_sums[:, 0], k_hat, k_sigma)
    d_proj = (
        jnp.stack([dq_raw, dk_raw, key_sums[:, 1]], axis=1)
        .astype(jnp.bfloat16)
        .reshape(query_rows, 3 * width_local)
    )
    d_proj_panel = collect_panel(d_proj, bit_count, bit_count, row_place, 0)
    input_partial = contract(d_proj_panel, w_in, 1, 1)
    input_grad = reduce_panel(input_partial, 0, bit_count, col_place, 1).astype(jnp.bfloat16)
    grad_in_part = contract(x_panel, d_proj_panel, 0, 0)
    grad_in, grad_out = (
        lax.psum_scatter(
            grad_in_part.astype(jnp.bfloat16), "depth", scatter_dimension=0, tiled=True
        ).astype(jnp.float32),
        lax.psum_scatter(
            grad_out_part.astype(jnp.bfloat16), "depth", scatter_dimension=0, tiled=True
        ).astype(jnp.float32),
    )
    qkv_grad = grad_in.astype(jnp.bfloat16).reshape(1, grad_in.shape[0], 3, heads_local, head_dim)
    out_proj_grad = grad_out.astype(jnp.bfloat16)[None]
    return (attention_out, input_grad, qkv_grad, out_proj_grad)


SIZES = [6]
HINT = 4096


def y_swap(value):
    return partner_2(value, "grid", 1)


def core_swap(value):
    return partner_2(value, "grid", 0)


def hint(flops, bytes_accessed, transcendentals):
    return pl.CostEstimate(
        flops=flops // HINT, bytes_accessed=bytes_accessed // HINT, transcendentals=transcendentals
    )


def params(*semantics):
    return pltpu.CompilerParams(dimension_semantics=semantics, vmem_limit_bytes=56 * 2**20)


def proj_kernel(place_ref, own_ref, other_ref, w_own_ref, w_other_ref, out_ref):
    heads = w_own_ref.shape[1]
    columns = [(part, head) for head in range(heads) for part in range(3)]
    w_own = jnp.concatenate([w_own_ref[part, head] for part, head in columns], axis=1)
    total = jnp.dot(own_ref[...], w_own, preferred_element_type=jnp.float32)
    w_other = jnp.concatenate([w_other_ref[part, head] for part, head in columns], axis=1)
    total += jnp.dot(other_ref[...], w_other, preferred_element_type=jnp.float32)
    out_ref[...] = total.astype(out_ref.dtype)


def project(place, x_own, x_other, weights, swap, start, heads, kind):
    rows, piece = x_own.shape
    head_dim = weights.shape[3]
    group = 2 if heads % 2 == 0 and start % 2 == 0 else 1
    if start % 3 == 0 and heads % 3 == 0:
        group = 3
    per_half = weights.shape[1] // 2 // group
    width = heads * 3 * head_dim

    def head_block(step, place):
        return (place[0] + swap) % 2 * per_half + start // group + step

    whole = pl.BlockSpec((rows, piece), lambda step, place: (0, 0))
    block = (3, group, piece, head_dim)
    return pl.pallas_call(
        proj_kernel,
        grid_spec=pltpu.PrefetchScalarGridSpec(
            num_scalar_prefetch=1,
            grid=(heads // group,),
            in_specs=[
                whole,
                whole,
                pl.BlockSpec(block, lambda step, place: (0, head_block(step, place), place[1], 0)),
                pl.BlockSpec(
                    block, lambda step, place: (0, head_block(step, place), 1 - place[1], 0)
                ),
            ],
            out_specs=pl.BlockSpec((rows, group * 3 * head_dim), lambda step, place: (0, step)),
        ),
        out_shape=jax.ShapeDtypeStruct((rows, width), kind),
        compiler_params=params("arbitrary"),
        cost_estimate=hint(
            flops=4 * rows * piece * width,
            bytes_accessed=4 * piece * width + 4 * rows * piece + 4 * rows * width,
            transcendentals=0,
        ),
        name="project",
    )(place, x_own, x_other, weights, weights)


def attention_kernel(scale, keep_ref, recv_ref, d_out_ref, att_ref, d_proj_ref):
    head_dim = d_out_ref.shape[1]
    low = jnp.bfloat16

    def part(index):
        columns = slice(index * head_dim, (index + 1) * head_dim)
        return keep_ref[:, columns] + recv_ref[:, columns].astype(jnp.float32)

    def dot(left, right, left_dim, right_dim):
        return contract(left, right, left_dim, right_dim)

    q_hat, q_sigma = normalize(part(0))
    k_hat, k_sigma = normalize(part(1))
    queries, keys, values = q_hat.astype(low), k_hat.astype(low), part(2).astype(low)
    d_out = d_out_ref[...]
    expo = jnp.exp(dot(queries, keys, 1, 1) * scale)
    probs = expo / jnp.sum(expo, axis=-1, keepdims=True)
    probs_low = probs.astype(low)
    att_ref[...] = dot(probs_low, values, 1, 0).astype(low)
    d_probs = dot(d_out, values, 1, 1)
    d_values = dot(probs_low, d_out, 0, 0)
    weighted = probs * d_probs
    d_scores = (weighted - probs * jnp.sum(weighted, axis=-1, keepdims=True)).astype(low)
    d_queries = dot(d_scores, keys, 1, 0) * scale
    d_keys = dot(d_scores, queries, 0, 0) * scale
    d_proj_ref[:, :head_dim] = normalize_back(d_queries, q_hat, q_sigma).astype(low)
    d_proj_ref[:, head_dim : 2 * head_dim] = normalize_back(d_keys, k_hat, k_sigma).astype(low)
    d_proj_ref[:, 2 * head_dim :] = d_values.astype(low)


def attend(keep, recv, d_attended, start, heads, head_dim):
    rows = keep.shape[0]
    triple = pl.BlockSpec((rows, 3 * head_dim), lambda head: (0, head))
    single = pl.BlockSpec((rows, head_dim), lambda head: (0, head))
    return pl.pallas_call(
        functools.partial(attention_kernel, head_dim ** (-0.5)),
        grid=(heads,),
        in_specs=[triple, triple, pl.BlockSpec((rows, head_dim), lambda head: (0, start + head))],
        out_specs=[single, triple],
        out_shape=[
            jax.ShapeDtypeStruct((rows, heads * head_dim), jnp.bfloat16),
            jax.ShapeDtypeStruct((rows, heads * 3 * head_dim), jnp.bfloat16),
        ],
        compiler_params=params("arbitrary"),
        cost_estimate=hint(
            flops=14 * heads * rows * rows * head_dim,
            bytes_accessed=28 * heads * rows * head_dim,
            transcendentals=0,
        ),
        name="attend",
    )(keep, recv, d_attended)


def input_kernel(place_ref, d_own_ref, d_other_ref, w_own_ref, w_other_ref, *refs):
    keep_ref, send_ref, acc_own_ref, acc_other_ref = refs
    step, steps = pl.program_id(0), pl.num_programs(0)
    heads = w_own_ref.shape[1]
    columns = [(part, head) for head in range(heads) for part in range(3)]

    @pl.when(step == 0)
    def _():
        acc_own_ref[...] = jnp.zeros_like(acc_own_ref)
        acc_other_ref[...] = jnp.zeros_like(acc_other_ref)

    def add(grads):
        for w_ref, acc_ref in ((w_own_ref, acc_own_ref), (w_other_ref, acc_other_ref)):
            w = jnp.concatenate([w_ref[part, head] for part, head in columns], axis=1)
            acc_ref[...] += contract(w, grads, 1, 1)

    @pl.when(step < steps // 2)
    def _():
        add(d_own_ref[...])

    @pl.when(step >= steps // 2)
    def _():
        add(d_other_ref[...])

    @pl.when(step == steps - 1)
    def _():
        keep_ref[...] = acc_own_ref[...].T
        send_ref[...] = acc_other_ref[...].T.astype(send_ref.dtype)


def input_terms(place, d_own, d_other, weights):
    rows, width = d_own.shape
    head_dim = weights.shape[3]
    piece = weights.shape[2] // 2
    heads_half = weights.shape[1] // 2
    group = 2 if heads_half % 2 == 0 else 1
    steps = heads_half // group

    def head_block(step, place):
        return (place[0] + step // steps) % 2 * steps + step % steps

    block = (3, group, piece, head_dim)
    total = pl.BlockSpec((rows, piece), lambda step, place: (0, 0))
    grads = (rows, group * 3 * head_dim)
    return pl.pallas_call(
        input_kernel,
        grid_spec=pltpu.PrefetchScalarGridSpec(
            num_scalar_prefetch=1,
            grid=(2 * steps,),
            in_specs=[
                pl.BlockSpec(grads, lambda step, place: (0, jnp.minimum(step, steps - 1))),
                pl.BlockSpec(grads, lambda step, place: (0, jnp.maximum(step - steps, 0))),
                pl.BlockSpec(block, lambda step, place: (0, head_block(step, place), place[1], 0)),
                pl.BlockSpec(
                    block, lambda step, place: (0, head_block(step, place), 1 - place[1], 0)
                ),
            ],
            out_specs=[total, total],
            scratch_shapes=[pltpu.VMEM((piece, rows), jnp.float32)] * 2,
        ),
        out_shape=[
            jax.ShapeDtypeStruct((rows, piece), jnp.float32),
            jax.ShapeDtypeStruct((rows, piece), jnp.bfloat16),
        ],
        compiler_params=params("arbitrary"),
        cost_estimate=hint(
            flops=8 * rows * piece * width,
            bytes_accessed=8 * piece * width + 10 * rows * piece,
            transcendentals=0,
        ),
        name="input_terms",
    )(place, d_own, d_other, weights, weights)


def weight_kernel(count, place_ref, x_own_ref, x_other_ref, *refs):
    slots, out_ref, x_sorted = refs[:count], refs[-2], refs[-1]
    heads, head_dim = out_ref.shape[1], out_ref.shape[3]
    patches, part_rows = x_own_ref.shape[0] // count, x_own_ref.shape[1]

    @pl.when(pl.program_id(0) == 0)
    def _():
        for side, x_ref in enumerate((x_own_ref, x_other_ref)):
            first = (place_ref[1] + side) % 2 * part_rows
            rows = pl.ds(pl.multiple_of(first, part_rows), part_rows)
            for slot in range(count):
                offset = pl.multiple_of(place_ref[2 + slot] * patches, patches)
                x_sorted[rows, slot * patches : (slot + 1) * patches] = x_ref[
                    pl.ds(offset, patches), :
                ].T

    grads = jnp.concatenate([slot_ref[...] for slot_ref in slots], axis=0)
    total = jnp.dot(x_sorted[...], grads, preferred_element_type=jnp.float32)
    for head in range(heads):
        for part in range(3):
            column = (head * 3 + part) * head_dim
            out_ref[part, head] = total[:, column : column + head_dim].astype(out_ref.dtype)


def weight_terms(place, x_own, x_other, slots, swap, start, shape, filled):
    count = len(slots)
    rows, width = slots[-1].shape
    block_rows = 2 * x_own.shape[1]
    head_dim = shape[3]
    heads = width // (3 * head_dim)
    group = 2 if heads % 2 == 0 and start % 2 == 0 else 1
    per_half = shape[1] // 2 // group
    part = pl.BlockSpec((rows, group * 3 * head_dim), lambda step, place: (0, step))
    filled = () if filled is None else (filled,)
    return pl.pallas_call(
        functools.partial(weight_kernel, count),
        grid_spec=pltpu.PrefetchScalarGridSpec(
            num_scalar_prefetch=1,
            grid=(heads // group,),
            in_specs=[pl.BlockSpec(x_own.shape, lambda step, place: (0, 0))] * 2
            + [part] * count
            + [pl.BlockSpec(memory_space=pl.ANY)] * len(filled),
            out_specs=pl.BlockSpec(
                (3, group, block_rows, head_dim),
                lambda step, place: (
                    0,
                    (place[0] + swap) % 2 * per_half + start // group + step,
                    0,
                    0,
                ),
            ),
            scratch_shapes=[pltpu.VMEM((block_rows, x_own.shape[0]), x_own.dtype)],
        ),
        out_shape=jax.ShapeDtypeStruct(shape, jnp.bfloat16),
        input_output_aliases={3 + count: 0} if filled else {},
        compiler_params=params("arbitrary"),
        cost_estimate=pl.CostEstimate(
            flops=2 * count * rows * block_rows * width,
            bytes_accessed=2 * count * rows * (block_rows + width) + 2 * block_rows * width,
            transcendentals=0,
        ),
        name="weight_terms",
    )(place, x_own, x_other, *slots, *filled)


def out_kernel(count, place_ref, att_ref, *refs):
    own, other, out_ref, att_turned = refs[:count], refs[count : 2 * count], refs[-2], refs[-1]

    @pl.when(pl.program_id(0) == 0)
    def _():
        att_turned[...] = att_ref[...].T

    def fill(slots):
        grads = jnp.concatenate([slot_ref[...] for slot_ref in slots], axis=0)
        total = jnp.dot(att_turned[...], grads, preferred_element_type=jnp.float32)
        out_ref[...] = total.astype(out_ref.dtype)

    half = pl.num_programs(0) // 2

    @pl.when(pl.program_id(0) < half)
    def _():
        fill(own)

    @pl.when(pl.program_id(0) >= half)
    def _():
        fill(other)


def out_terms(place, att_slots, own, other):
    count = len(own)
    width = own[0].shape[1]
    steps = 2 if width % 256 == 0 else 1
    block = width // steps
    rows, block_rows = att_slots.shape
    return pl.pallas_call(
        functools.partial(out_kernel, count),
        grid_spec=pltpu.PrefetchScalarGridSpec(
            num_scalar_prefetch=1,
            grid=(2 * steps,),
            in_specs=[pl.BlockSpec((rows, block_rows), lambda step, place: (0, 0))]
            + [
                pl.BlockSpec(
                    (slot.shape[0], block),
                    lambda step, place: (0, jnp.minimum(step, steps - 1)),
                )
                for slot in own
            ]
            + [
                pl.BlockSpec(
                    (slot.shape[0], block),
                    lambda step, place: (0, jnp.maximum(step - steps, 0)),
                )
                for slot in other
            ],
            out_specs=pl.BlockSpec(
                (block_rows, block),
                lambda step, place: (
                    0,
                    (place[1] + step // steps) % 2 * steps + step % steps,
                ),
            ),
            scratch_shapes=[pltpu.VMEM((block_rows, rows), att_slots.dtype)],
        ),
        out_shape=jax.ShapeDtypeStruct((block_rows, 2 * width), jnp.bfloat16),
        compiler_params=params("arbitrary"),
        cost_estimate=hint(
            flops=4 * rows * block_rows * width,
            bytes_accessed=4 * rows * width + 2 * block_rows * (rows + 2 * width),
            transcendentals=0,
        ),
        name="out_terms",
    )(place, att_slots, *own, *other)


def output_kernel(place_ref, own_ref, other_ref, v_own_ref, v_other_ref, keep_ref, send_ref):
    total = jnp.dot(own_ref[...], v_own_ref[...], preferred_element_type=jnp.float32)
    total += jnp.dot(other_ref[...], v_other_ref[...], preferred_element_type=jnp.float32)

    @pl.when(pl.program_id(0) == 0)
    def _():
        send_ref[...] = total.astype(send_ref.dtype)

    @pl.when(pl.program_id(0) == 1)
    def _():
        keep_ref[...] = total


def output_terms(place, att_own, att_other, w_back):
    rows, half = att_own.shape
    last = att_other.shape[1] // half - 1
    piece = w_back.shape[1] // 2
    whole = pl.BlockSpec((rows, half), lambda step, place: (0, 0))
    result = pl.BlockSpec((rows, piece), lambda step, place: (0, 0))
    return pl.pallas_call(
        output_kernel,
        grid_spec=pltpu.PrefetchScalarGridSpec(
            num_scalar_prefetch=1,
            grid=(2,),
            in_specs=[
                whole,
                pl.BlockSpec((rows, half), lambda step, place: (0, last)),
                pl.BlockSpec(
                    (half, piece), lambda step, place: (place[0], (place[1] + 1 + step) % 2)
                ),
                pl.BlockSpec(
                    (half, piece), lambda step, place: (1 - place[0], (place[1] + 1 + step) % 2)
                ),
            ],
            out_specs=[result, result],
        ),
        out_shape=[
            jax.ShapeDtypeStruct((rows, piece), jnp.float32),
            jax.ShapeDtypeStruct((rows, piece), jnp.bfloat16),
        ],
        compiler_params=params("arbitrary"),
        cost_estimate=hint(
            flops=8 * rows * half * piece,
            bytes_accessed=8 * half * piece + 4 * rows * half + 6 * rows * piece,
            transcendentals=0,
        ),
        name="output_terms",
    )(place, att_own, att_other, w_back, w_back)


def ordered(place, own, other, along):
    return jnp.where(
        place == 0,
        jnp.concatenate([own, other], along),
        jnp.concatenate([other, own], along),
    )


def line_step(upper, lower, axis):
    count = lax.axis_size(axis)
    step = len(upper)
    upper.append(lax.ppermute(upper[-1], axis, [(d + 1, d) for d in range(count - step)]))
    lower.append(lax.ppermute(lower[-1], axis, [(d - 1, d) for d in range(step, count)]))


def together(*groups):
    flat, tree = jax.tree.flatten(groups)
    return jax.tree.unflatten(tree, lax.optimization_barrier(flat))


def by_offset(upper, lower, axis):
    count = lax.axis_size(axis)
    place = lax.axis_index(axis)
    return [
        jnp.where(place + slot < count, upper[slot], lower[count - slot])
        for slot in range(1, count)
    ]


def arrivals(count):
    table = []
    for place in range(count):
        found = []
        for step in range(1, count):
            found += [(0, step)] * (place + step < count) + [(1, step)] * (place >= step)
        if place >= count // 2:
            found.sort(key=lambda item: (item[1], -item[0]))
        table.append(found)
    return table


def pick_arrival(upper, lower, index, table, axis):
    place = lax.axis_index(axis)
    picked = None
    for other, found in enumerate(table):
        side, step = found[index]
        source = (upper, lower)[side][step]
        picked = source if picked is None else jnp.where(place == other, source, picked)
    return picked


def send_slots(blocks_of, axis):
    count = lax.axis_size(axis)
    place = lax.axis_index(axis)
    slots = [blocks_of(place)]
    for slot in range(1, count):
        target = (place + count - slot) % count
        pairs = [(d, (d + count - slot) % count) for d in range(count)]
        slots.append(lax.ppermute(blocks_of(target), axis, pairs))
    return slots


def local_heads(patch_rows, qkv_blocks, out_blocks, out_grad):
    depth = lax.axis_size("depth")
    grid_index = lax.axis_index("grid")
    row_place, col_place = grid_index // 2, grid_index % 2
    depth_place = lax.axis_index("depth")
    table = arrivals(depth)
    offsets = [0] + [
        sum(
            jnp.where(depth_place == d, (step if side == 0 else depth - step), 0)
            for d, (side, step) in enumerate(table[d][index] for d in range(depth))
        )
        for index in range(depth - 1)
    ]
    place = jnp.stack([row_place, col_place, *offsets]).astype(jnp.int32)
    heads_local, head_dim = qkv_blocks.shape[3:]
    heads_half = heads_local // 2
    half = heads_half * head_dim
    weights = qkv_blocks[0].transpose(1, 2, 0, 3)
    w_back = out_blocks[0]
    low = jnp.bfloat16
    sizes = SIZES if heads_half == sum(SIZES) else [heads_half]
    chunks = [(sum(sizes[:index]), size) for index, size in enumerate(sizes)]

    x_other = core_swap(patch_rows)
    g_other = core_swap(out_grad)
    received = []
    for start, heads in chunks:
        send = project(place, patch_rows, x_other, weights, 1, start, heads, low)
        received.append(y_swap(send))
    g_line = ([out_grad], [out_grad])
    line_step(*g_line, "depth")
    line_step(*g_line, "depth")
    grad_panel = ordered(col_place, out_grad, g_other, 1)
    d_att_partial = contract(grad_panel, w_back, 1, 1)
    d_att_send = lax.dynamic_slice_in_dim(d_att_partial, (1 - row_place) * half, half, 1)
    d_att_keep = lax.dynamic_slice_in_dim(d_att_partial, row_place * half, half, 1)
    d_attended = (d_att_keep + y_swap(d_att_send.astype(low)).astype(jnp.float32)).astype(low)

    x_panel = ordered(col_place, patch_rows, x_other, 1)
    block_rows = x_panel.shape[1] // depth
    part_rows = block_rows // 2
    x_parts = send_slots(
        lambda target: lax.dynamic_slice_in_dim(
            x_panel, target * block_rows + col_place * part_rows, part_rows, 1
        ),
        "depth",
    )

    shape = (3, heads_local, block_rows, head_dim)
    attended, d_proj = [], []
    for (start, heads), recv in zip(chunks, received):
        keep = project(place, patch_rows, x_other, weights, 0, start, heads, jnp.float32)
        parts = attend(keep, recv, d_attended, start, heads, head_dim)
        attended.append(parts[0])
        d_proj.append(parts[1])
    attended, d_proj = jnp.concatenate(attended, axis=1), jnp.concatenate(d_proj, axis=1)

    d_proj, attended, g_line, x_parts = together(d_proj, attended, g_line, x_parts)
    upper, lower = [d_proj], [d_proj]
    own, other = [d_proj], [y_swap(jnp.concatenate([d_proj, attended], axis=1))]

    line_step(upper, lower, "depth")
    slot = pick_arrival(upper, lower, 0, table, "depth")
    x_own = jnp.concatenate(x_parts, axis=0)
    x_swapped = core_swap(x_own)
    upper, lower, slot, other, x_own, x_swapped, attended = together(
        upper, lower, slot, other, x_own, x_swapped, attended
    )
    attended_panel = ordered(row_place, attended, other[0][:, d_proj.shape[1] :], 1)
    own.append(slot)
    other.append(y_swap(slot))

    line_step(upper, lower, "depth")
    slot = pick_arrival(upper, lower, 1, table, "depth")
    input_keep, input_send = input_terms(place, own[0], other[0], weights)
    out_keep, out_send = output_terms(place, attended, other[0], w_back)
    upper, lower, slot, other, input_keep, input_send, out_keep, out_send, attended_panel = together(
        upper, lower, slot, other, input_keep, input_send, out_keep, out_send, attended_panel
    )
    own.append(slot)
    other.append(y_swap(slot))

    line_step(upper, lower, "depth")
    input_grad = (input_keep + core_swap(input_send).astype(jnp.float32)).astype(low)
    slot = pick_arrival(upper, lower, 2, table, "depth")
    attention_out = (out_keep + core_swap(out_send).astype(jnp.float32)).astype(low)
    slot, x_own, input_grad, attended_panel, g_line = together(
        slot, x_own, input_grad, attended_panel, g_line
    )
    own.append(slot)
    other.append(y_swap(slot))

    line_step(*g_line, "depth")
    grad_rows = w_back.shape[0] // depth
    a_slots = send_slots(
        lambda target: lax.dynamic_slice_in_dim(
            attended_panel, target * grad_rows, grad_rows, 1
        ),
        "depth",
    )
    filled = weight_terms(place, x_own, x_swapped, own, 0, 0, shape, None)
    other, g_line, a_slots, attention_out, filled = together(
        other, g_line, a_slots, attention_out, filled
    )

    g_far = jnp.concatenate(by_offset(*g_line, "depth"), axis=0)
    g_far_other = core_swap(g_far)
    filled = weight_terms(place, x_own, x_swapped, other, 1, 0, shape, filled)
    out_proj_grad = out_terms(
        place,
        jnp.concatenate(a_slots, axis=0),
        [out_grad, g_far],
        [g_other, g_far_other],
    )
    qkv_grad = filled.transpose(2, 0, 1, 3)[None]
    return (attention_out, input_grad, qkv_grad, out_proj_grad[None])


def local_any(patch_rows, qkv_blocks, out_blocks, out_grad):
    by_heads = (
        lax.axis_size("grid") == 4
        and qkv_blocks.shape[3] % 2 == 0
        and patch_rows.shape[0] == PATCHES
        and qkv_blocks.shape[1] % (2 * lax.axis_size("depth")) == 0
        and out_blocks.shape[1] % lax.axis_size("depth") == 0
        and lax.axis_size("depth") == 4
    )
    body = local_heads if by_heads else local
    return body(patch_rows, qkv_blocks, out_blocks, out_grad)


def solution(mesh):
    return jax.shard_map(
        local_any,
        mesh=mesh,
        in_specs=(
            P(("groups", "depth"), "grid"),
            P("grid", None, None, None, None),
            P("grid", None, None),
            P(("groups", "depth"), "grid"),
        ),
        out_specs=(
            P(("groups", "depth"), "grid"),
            P(("groups", "depth"), "grid"),
            P(("groups", "grid"), "depth", None, None, None),
            P(("groups", "grid"), "depth", None),
        ),
        check_vma=False,
    )
```

```python
import functools
import math

import jax
import jax.numpy as jnp
from jax import lax
from jax.experimental import pallas as pl
from jax.experimental.pallas import tpu as pltpu
from jax.sharding import PartitionSpec as P

PATCHES = 256


eps = 1e-06


def partner_2(value, axis, stride):
    mask = 2**stride
    pairs = [(source, source ^ mask) for source in range(lax.axis_size(axis))]
    return lax.ppermute(value, axis, pairs)


def normalize(vectors):
    center = vectors - jnp.mean(vectors, axis=-1, keepdims=True)
    spread = jnp.mean(center * center, axis=-1, keepdims=True)
    sigma = jnp.sqrt(spread + eps)
    return (center / sigma, sigma)


def normalize_back(grads, normed, sigma):
    first_mean = jnp.mean(grads, axis=-1, keepdims=True)
    second_mean = jnp.mean(grads * normed, axis=-1, keepdims=True)
    return (grads - first_mean - normed * second_mean) / sigma


def collect_panel(pieces, first_bit, count, position, along):
    for section in range(count):
        partner = partner_2(pieces, "grid", first_bit + section)
        higher = position >> section & 1
        pieces = jnp.where(
            higher == 1,
            jnp.concatenate([partner, pieces], along),
            jnp.concatenate([pieces, partner], along),
        )
    return pieces


def reduce_panel(partial_sum, first_bit, count, position, along):
    for section in reversed(range(count)):
        half_size = partial_sum.shape[along] // 2
        higher = position >> section & 1
        kept = lax.dynamic_slice_in_dim(partial_sum, higher * half_size, half_size, along)
        outgoing = lax.dynamic_slice_in_dim(partial_sum, (1 - higher) * half_size, half_size, along)
        partial_sum = kept + partner_2(
            outgoing.astype(jnp.bfloat16), "grid", first_bit + section
        ).astype(outgoing.dtype)
    return partial_sum


def contract(left, right, left_dim, right_dim):
    return lax.dot_general(
        left, right, (((left_dim,), (right_dim,)), ((), ())), preferred_element_type=jnp.float32
    )


def local(patch_rows, qkv_blocks, out_blocks, out_grad):
    side = math.isqrt(lax.axis_size("grid"))
    bit_count = side.bit_length() - 1
    grid_index = lax.axis_index("grid")
    row_place = grid_index // side
    col_place = grid_index % side
    slice_rows = patch_rows.shape[0]
    block_width = qkv_blocks.shape[1]
    heads_local = qkv_blocks.shape[3]
    head_dim = qkv_blocks.shape[4]
    width_local = heads_local * head_dim
    query_rows = slice_rows // side
    scale = head_dim ** (-0.5)
    x_panel = collect_panel(patch_rows, 0, bit_count, col_place, 1)
    w_in = qkv_blocks[0].reshape(block_width, 3 * width_local)
    partial_proj = jnp.dot(x_panel, w_in, preferred_element_type=jnp.float32)
    proj_local = reduce_panel(partial_proj, bit_count, bit_count, row_place, 0)
    proj_local = proj_local.reshape(query_rows, 3, heads_local, head_dim)
    query_raw = proj_local[:, 0]
    k_hat, k_sigma = normalize(proj_local[:, 1])
    kv_local = jnp.stack(
        [k_hat.astype(jnp.bfloat16), proj_local[:, 2].astype(jnp.bfloat16)], axis=1
    )
    kv_gathered = collect_panel(kv_local, bit_count, bit_count, row_place, 0)
    keys_all = kv_gathered[:, 0]
    values_all = kv_gathered[:, 1]
    q_hat, q_sigma = normalize(query_raw)
    queries = q_hat.astype(jnp.bfloat16)
    group_count = max(1, query_rows // PATCHES)
    key_rows = max(query_rows, PATCHES)
    group_shape = (group_count, key_rows // group_count, heads_local, head_dim)
    keys = keys_all.reshape(group_shape)
    values = values_all.reshape(group_shape)
    query_group = queries.reshape(group_count, query_rows // group_count, heads_local, head_dim)
    scores = (
        jnp.einsum("gqhe,gkhe->ghqk", query_group, keys, preferred_element_type=jnp.float32) * scale
    )
    expo = jnp.exp(scores)
    probs = expo / jnp.sum(expo, axis=-1, keepdims=True)
    probs_low = probs.astype(jnp.bfloat16)
    attended = jnp.einsum("ghqk,gkhe->gqhe", probs_low, values, preferred_element_type=jnp.float32)
    attended = attended.astype(jnp.bfloat16).reshape(query_rows, width_local)
    attended_panel = collect_panel(attended, bit_count, bit_count, row_place, 0)
    w_back = out_blocks[0]
    out_partial = jnp.dot(attended_panel, w_back, preferred_element_type=jnp.float32)
    attention_out = reduce_panel(out_partial, 0, bit_count, col_place, 1).astype(jnp.bfloat16)
    grad_panel = collect_panel(out_grad, 0, bit_count, col_place, 1)
    d_att_partial = contract(grad_panel, w_back, 1, 1)
    d_attended = reduce_panel(d_att_partial, bit_count, bit_count, row_place, 0).astype(
        jnp.bfloat16
    )
    d_attended = d_attended.reshape(group_count, query_rows // group_count, heads_local, head_dim)
    grad_out_part = contract(attended_panel, grad_panel, 0, 0)
    d_probs = jnp.einsum("gqhe,gkhe->ghqk", d_attended, values, preferred_element_type=jnp.float32)
    d_values = jnp.einsum(
        "ghqk,gqhe->gkhe", probs_low, d_attended, preferred_element_type=jnp.float32
    )
    d_scores = (probs * (d_probs - jnp.sum(probs * d_probs, axis=-1, keepdims=True))).astype(
        jnp.bfloat16
    )
    d_queries = (
        jnp.einsum("ghqk,gkhe->gqhe", d_scores, keys, preferred_element_type=jnp.float32) * scale
    )
    d_keys = (
        jnp.einsum("ghqk,gqhe->gkhe", d_scores, query_group, preferred_element_type=jnp.float32)
        * scale
    )
    key_terms = jnp.stack(
        [
            d_keys.reshape(key_rows, heads_local, head_dim),
            d_values.reshape(key_rows, heads_local, head_dim),
        ],
        axis=1,
    )
    key_sums = reduce_panel(key_terms, bit_count, bit_count, row_place, 0)
    dq_raw = normalize_back(d_queries.reshape(query_rows, heads_local, head_dim), q_hat, q_sigma)
    dk_raw = normalize_back(key_sums[:, 0], k_hat, k_sigma)
    d_proj = (
        jnp.stack([dq_raw, dk_raw, key_sums[:, 1]], axis=1)
        .astype(jnp.bfloat16)
        .reshape(query_rows, 3 * width_local)
    )
    d_proj_panel = collect_panel(d_proj, bit_count, bit_count, row_place, 0)
    input_partial = contract(d_proj_panel, w_in, 1, 1)
    input_grad = reduce_panel(input_partial, 0, bit_count, col_place, 1).astype(jnp.bfloat16)
    grad_in_part = contract(x_panel, d_proj_panel, 0, 0)
    grad_in, grad_out = (
        lax.psum_scatter(
            grad_in_part.astype(jnp.bfloat16), "depth", scatter_dimension=0, tiled=True
        ).astype(jnp.float32),
        lax.psum_scatter(
            grad_out_part.astype(jnp.bfloat16), "depth", scatter_dimension=0, tiled=True
        ).astype(jnp.float32),
    )
    qkv_grad = grad_in.astype(jnp.bfloat16).reshape(1, grad_in.shape[0], 3, heads_local, head_dim)
    out_proj_grad = grad_out.astype(jnp.bfloat16)[None]
    return (attention_out, input_grad, qkv_grad, out_proj_grad)


SIZES = [6]
HINT = 4096


def y_swap(value):
    return partner_2(value, "grid", 1)


def core_swap(value):
    return partner_2(value, "grid", 0)


def hint(flops, bytes_accessed, transcendentals):
    return pl.CostEstimate(
        flops=flops // HINT, bytes_accessed=bytes_accessed // HINT, transcendentals=transcendentals
    )


def params(*semantics):
    return pltpu.CompilerParams(dimension_semantics=semantics, vmem_limit_bytes=56 * 2**20)


def proj_kernel(place_ref, own_ref, other_ref, w_own_ref, w_other_ref, out_ref):
    heads = w_own_ref.shape[1]
    columns = [(part, head) for head in range(heads) for part in range(3)]
    w_own = jnp.concatenate([w_own_ref[part, head] for part, head in columns], axis=1)
    total = jnp.dot(own_ref[...], w_own, preferred_element_type=jnp.float32)
    w_other = jnp.concatenate([w_other_ref[part, head] for part, head in columns], axis=1)
    total += jnp.dot(other_ref[...], w_other, preferred_element_type=jnp.float32)
    out_ref[...] = total.astype(out_ref.dtype)


def project(place, x_own, x_other, weights, swap, start, heads, kind):
    rows, piece = x_own.shape
    head_dim = weights.shape[3]
    group = 2 if heads % 2 == 0 and start % 2 == 0 else 1
    if start % 3 == 0 and heads % 3 == 0:
        group = 3
    per_half = weights.shape[1] // 2 // group
    width = heads * 3 * head_dim

    def head_block(step, place):
        return (place[0] + swap) % 2 * per_half + start // group + step

    whole = pl.BlockSpec((rows, piece), lambda step, place: (0, 0))
    block = (3, group, piece, head_dim)
    return pl.pallas_call(
        proj_kernel,
        grid_spec=pltpu.PrefetchScalarGridSpec(
            num_scalar_prefetch=1,
            grid=(heads // group,),
            in_specs=[
                whole,
                whole,
                pl.BlockSpec(block, lambda step, place: (0, head_block(step, place), place[1], 0)),
                pl.BlockSpec(
                    block, lambda step, place: (0, head_block(step, place), 1 - place[1], 0)
                ),
            ],
            out_specs=pl.BlockSpec((rows, group * 3 * head_dim), lambda step, place: (0, step)),
        ),
        out_shape=jax.ShapeDtypeStruct((rows, width), kind),
        compiler_params=params("arbitrary"),
        cost_estimate=hint(
            flops=4 * rows * piece * width,
            bytes_accessed=4 * piece * width + 4 * rows * piece + 4 * rows * width,
            transcendentals=0,
        ),
        name="project",
    )(place, x_own, x_other, weights, weights)


def attention_kernel(scale, keep_ref, recv_ref, d_out_ref, att_ref, d_proj_ref):
    head_dim = d_out_ref.shape[1]
    low = jnp.bfloat16

    def part(index):
        columns = slice(index * head_dim, (index + 1) * head_dim)
        return keep_ref[:, columns] + recv_ref[:, columns].astype(jnp.float32)

    def dot(left, right, left_dim, right_dim):
        return contract(left, right, left_dim, right_dim)

    q_hat, q_sigma = normalize(part(0))
    k_hat, k_sigma = normalize(part(1))
    queries, keys, values = q_hat.astype(low), k_hat.astype(low), part(2).astype(low)
    d_out = d_out_ref[...]
    expo = jnp.exp(dot(queries, keys, 1, 1) * scale)
    probs = expo / jnp.sum(expo, axis=-1, keepdims=True)
    probs_low = probs.astype(low)
    att_ref[...] = dot(probs_low, values, 1, 0).astype(low)
    d_probs = dot(d_out, values, 1, 1)
    d_values = dot(probs_low, d_out, 0, 0)
    weighted = probs * d_probs
    d_scores = (weighted - probs * jnp.sum(weighted, axis=-1, keepdims=True)).astype(low)
    d_queries = dot(d_scores, keys, 1, 0) * scale
    d_keys = dot(d_scores, queries, 0, 0) * scale
    d_proj_ref[:, :head_dim] = normalize_back(d_queries, q_hat, q_sigma).astype(low)
    d_proj_ref[:, head_dim : 2 * head_dim] = normalize_back(d_keys, k_hat, k_sigma).astype(low)
    d_proj_ref[:, 2 * head_dim :] = d_values.astype(low)


def attend(keep, recv, d_attended, start, heads, head_dim):
    rows = keep.shape[0]
    triple = pl.BlockSpec((rows, 3 * head_dim), lambda head: (0, head))
    single = pl.BlockSpec((rows, head_dim), lambda head: (0, head))
    return pl.pallas_call(
        functools.partial(attention_kernel, head_dim ** (-0.5)),
        grid=(heads,),
        in_specs=[triple, triple, pl.BlockSpec((rows, head_dim), lambda head: (0, start + head))],
        out_specs=[single, triple],
        out_shape=[
            jax.ShapeDtypeStruct((rows, heads * head_dim), jnp.bfloat16),
            jax.ShapeDtypeStruct((rows, heads * 3 * head_dim), jnp.bfloat16),
        ],
        compiler_params=params("arbitrary"),
        cost_estimate=hint(
            flops=14 * heads * rows * rows * head_dim,
            bytes_accessed=28 * heads * rows * head_dim,
            transcendentals=0,
        ),
        name="attend",
    )(keep, recv, d_attended)


def input_kernel(place_ref, d_own_ref, d_other_ref, w_own_ref, w_other_ref, *refs):
    keep_ref, send_ref, acc_own_ref, acc_other_ref = refs
    step, steps = pl.program_id(0), pl.num_programs(0)
    heads = w_own_ref.shape[1]
    columns = [(part, head) for head in range(heads) for part in range(3)]

    @pl.when(step == 0)
    def _():
        acc_own_ref[...] = jnp.zeros_like(acc_own_ref)
        acc_other_ref[...] = jnp.zeros_like(acc_other_ref)

    def add(grads):
        for w_ref, acc_ref in ((w_own_ref, acc_own_ref), (w_other_ref, acc_other_ref)):
            w = jnp.concatenate([w_ref[part, head] for part, head in columns], axis=1)
            acc_ref[...] += contract(w, grads, 1, 1)

    @pl.when(step < steps // 2)
    def _():
        add(d_own_ref[...])

    @pl.when(step >= steps // 2)
    def _():
        add(d_other_ref[...])

    @pl.when(step == steps - 1)
    def _():
        keep_ref[...] = acc_own_ref[...].T
        send_ref[...] = acc_other_ref[...].T.astype(send_ref.dtype)


def input_terms(place, d_own, d_other, weights):
    rows, width = d_own.shape
    head_dim = weights.shape[3]
    piece = weights.shape[2] // 2
    heads_half = weights.shape[1] // 2
    group = 2 if heads_half % 2 == 0 else 1
    steps = heads_half // group

    def head_block(step, place):
        return (place[0] + step // steps) % 2 * steps + step % steps

    block = (3, group, piece, head_dim)
    total = pl.BlockSpec((rows, piece), lambda step, place: (0, 0))
    grads = (rows, group * 3 * head_dim)
    return pl.pallas_call(
        input_kernel,
        grid_spec=pltpu.PrefetchScalarGridSpec(
            num_scalar_prefetch=1,
            grid=(2 * steps,),
            in_specs=[
                pl.BlockSpec(grads, lambda step, place: (0, jnp.minimum(step, steps - 1))),
                pl.BlockSpec(grads, lambda step, place: (0, jnp.maximum(step - steps, 0))),
                pl.BlockSpec(block, lambda step, place: (0, head_block(step, place), place[1], 0)),
                pl.BlockSpec(
                    block, lambda step, place: (0, head_block(step, place), 1 - place[1], 0)
                ),
            ],
            out_specs=[total, total],
            scratch_shapes=[pltpu.VMEM((piece, rows), jnp.float32)] * 2,
        ),
        out_shape=[
            jax.ShapeDtypeStruct((rows, piece), jnp.float32),
            jax.ShapeDtypeStruct((rows, piece), jnp.bfloat16),
        ],
        compiler_params=params("arbitrary"),
        cost_estimate=hint(
            flops=8 * rows * piece * width,
            bytes_accessed=8 * piece * width + 10 * rows * piece,
            transcendentals=0,
        ),
        name="input_terms",
    )(place, d_own, d_other, weights, weights)


def weight_kernel(count, place_ref, x_own_ref, x_other_ref, *refs):
    slots, out_ref, x_sorted = refs[:count], refs[-2], refs[-1]
    heads, head_dim = out_ref.shape[1], out_ref.shape[3]
    patches, part_rows = x_own_ref.shape[0] // count, x_own_ref.shape[1]

    @pl.when(pl.program_id(0) == 0)
    def _():
        for side, x_ref in enumerate((x_own_ref, x_other_ref)):
            first = (place_ref[1] + side) % 2 * part_rows
            rows = pl.ds(pl.multiple_of(first, part_rows), part_rows)
            for slot in range(count):
                offset = pl.multiple_of(place_ref[2 + slot] * patches, patches)
                x_sorted[rows, slot * patches : (slot + 1) * patches] = x_ref[
                    pl.ds(offset, patches), :
                ].T

    grads = jnp.concatenate([slot_ref[...] for slot_ref in slots], axis=0)
    total = jnp.dot(x_sorted[...], grads, preferred_element_type=jnp.float32)
    for head in range(heads):
        for part in range(3):
            column = (head * 3 + part) * head_dim
            out_ref[part, head] = total[:, column : column + head_dim].astype(out_ref.dtype)


def weight_terms(place, x_own, x_other, slots, swap, start, shape, filled):
    count = len(slots)
    rows, width = slots[-1].shape
    block_rows = 2 * x_own.shape[1]
    head_dim = shape[3]
    heads = width // (3 * head_dim)
    group = 2 if heads % 2 == 0 and start % 2 == 0 else 1
    per_half = shape[1] // 2 // group
    part = pl.BlockSpec((rows, group * 3 * head_dim), lambda step, place: (0, step))
    filled = () if filled is None else (filled,)
    return pl.pallas_call(
        functools.partial(weight_kernel, count),
        grid_spec=pltpu.PrefetchScalarGridSpec(
            num_scalar_prefetch=1,
            grid=(heads // group,),
            in_specs=[pl.BlockSpec(x_own.shape, lambda step, place: (0, 0))] * 2
            + [part] * count
            + [pl.BlockSpec(memory_space=pl.ANY)] * len(filled),
            out_specs=pl.BlockSpec(
                (3, group, block_rows, head_dim),
                lambda step, place: (
                    0,
                    (place[0] + swap) % 2 * per_half + start // group + step,
                    0,
                    0,
                ),
            ),
            scratch_shapes=[pltpu.VMEM((block_rows, x_own.shape[0]), x_own.dtype)],
        ),
        out_shape=jax.ShapeDtypeStruct(shape, jnp.bfloat16),
        input_output_aliases={3 + count: 0} if filled else {},
        compiler_params=params("arbitrary"),
        cost_estimate=pl.CostEstimate(
            flops=2 * count * rows * block_rows * width,
            bytes_accessed=2 * count * rows * (block_rows + width) + 2 * block_rows * width,
            transcendentals=0,
        ),
        name="weight_terms",
    )(place, x_own, x_other, *slots, *filled)


def out_kernel(count, place_ref, att_ref, *refs):
    own, other, out_ref, att_turned = refs[:count], refs[count : 2 * count], refs[-2], refs[-1]

    @pl.when(pl.program_id(0) == 0)
    def _():
        att_turned[...] = att_ref[...].T

    def fill(slots):
        grads = jnp.concatenate([slot_ref[...] for slot_ref in slots], axis=0)
        total = jnp.dot(att_turned[...], grads, preferred_element_type=jnp.float32)
        out_ref[...] = total.astype(out_ref.dtype)

    half = pl.num_programs(0) // 2

    @pl.when(pl.program_id(0) < half)
    def _():
        fill(own)

    @pl.when(pl.program_id(0) >= half)
    def _():
        fill(other)


def out_terms(place, att_slots, own, other):
    count = len(own)
    width = own[0].shape[1]
    steps = 2 if width % 256 == 0 else 1
    block = width // steps
    rows, block_rows = att_slots.shape
    return pl.pallas_call(
        functools.partial(out_kernel, count),
        grid_spec=pltpu.PrefetchScalarGridSpec(
            num_scalar_prefetch=1,
            grid=(2 * steps,),
            in_specs=[pl.BlockSpec((rows, block_rows), lambda step, place: (0, 0))]
            + [
                pl.BlockSpec(
                    (slot.shape[0], block),
                    lambda step, place: (0, jnp.minimum(step, steps - 1)),
                )
                for slot in own
            ]
            + [
                pl.BlockSpec(
                    (slot.shape[0], block),
                    lambda step, place: (0, jnp.maximum(step - steps, 0)),
                )
                for slot in other
            ],
            out_specs=pl.BlockSpec(
                (block_rows, block),
                lambda step, place: (
                    0,
                    (place[1] + step // steps) % 2 * steps + step % steps,
                ),
            ),
            scratch_shapes=[pltpu.VMEM((block_rows, rows), att_slots.dtype)],
        ),
        out_shape=jax.ShapeDtypeStruct((block_rows, 2 * width), jnp.bfloat16),
        compiler_params=params("arbitrary"),
        cost_estimate=hint(
            flops=4 * rows * block_rows * width,
            bytes_accessed=4 * rows * width + 2 * block_rows * (rows + 2 * width),
            transcendentals=0,
        ),
        name="out_terms",
    )(place, att_slots, *own, *other)


def output_kernel(place_ref, own_ref, other_ref, v_own_ref, v_other_ref, keep_ref, send_ref):
    total = jnp.dot(own_ref[...], v_own_ref[...], preferred_element_type=jnp.float32)
    total += jnp.dot(other_ref[...], v_other_ref[...], preferred_element_type=jnp.float32)

    @pl.when(pl.program_id(0) == 0)
    def _():
        send_ref[...] = total.astype(send_ref.dtype)

    @pl.when(pl.program_id(0) == 1)
    def _():
        keep_ref[...] = total


def output_terms(place, att_own, att_other, w_back):
    rows, half = att_own.shape
    last = att_other.shape[1] // half - 1
    piece = w_back.shape[1] // 2
    whole = pl.BlockSpec((rows, half), lambda step, place: (0, 0))
    result = pl.BlockSpec((rows, piece), lambda step, place: (0, 0))
    return pl.pallas_call(
        output_kernel,
        grid_spec=pltpu.PrefetchScalarGridSpec(
            num_scalar_prefetch=1,
            grid=(2,),
            in_specs=[
                whole,
                pl.BlockSpec((rows, half), lambda step, place: (0, last)),
                pl.BlockSpec(
                    (half, piece), lambda step, place: (place[0], (place[1] + 1 + step) % 2)
                ),
                pl.BlockSpec(
                    (half, piece), lambda step, place: (1 - place[0], (place[1] + 1 + step) % 2)
                ),
            ],
            out_specs=[result, result],
        ),
        out_shape=[
            jax.ShapeDtypeStruct((rows, piece), jnp.float32),
            jax.ShapeDtypeStruct((rows, piece), jnp.bfloat16),
        ],
        compiler_params=params("arbitrary"),
        cost_estimate=hint(
            flops=8 * rows * half * piece,
            bytes_accessed=8 * half * piece + 4 * rows * half + 6 * rows * piece,
            transcendentals=0,
        ),
        name="output_terms",
    )(place, att_own, att_other, w_back, w_back)


def ordered(place, own, other, along):
    return jnp.where(
        place == 0,
        jnp.concatenate([own, other], along),
        jnp.concatenate([other, own], along),
    )


def line_step(upper, lower, axis):
    count = lax.axis_size(axis)
    step = len(upper)
    upper.append(lax.ppermute(upper[-1], axis, [(d + 1, d) for d in range(count - step)]))
    lower.append(lax.ppermute(lower[-1], axis, [(d - 1, d) for d in range(step, count)]))


def together(*groups):
    flat, tree = jax.tree.flatten(groups)
    return jax.tree.unflatten(tree, lax.optimization_barrier(flat))


def by_offset(upper, lower, axis):
    count = lax.axis_size(axis)
    place = lax.axis_index(axis)
    return [
        jnp.where(place + slot < count, upper[slot], lower[count - slot])
        for slot in range(1, count)
    ]


def arrivals(count):
    table = []
    for place in range(count):
        found = []
        for step in range(1, count):
            found += [(0, step)] * (place + step < count) + [(1, step)] * (place >= step)
        if place >= count // 2:
            found.sort(key=lambda item: (item[1], -item[0]))
        table.append(found)
    return table


def pick_arrival(upper, lower, index, table, axis):
    place = lax.axis_index(axis)
    picked = None
    for other, found in enumerate(table):
        side, step = found[index]
        source = (upper, lower)[side][step]
        picked = source if picked is None else jnp.where(place == other, source, picked)
    return picked


def send_slots(blocks_of, axis):
    count = lax.axis_size(axis)
    place = lax.axis_index(axis)
    slots = [blocks_of(place)]
    for slot in range(1, count):
        target = (place + count - slot) % count
        pairs = [(d, (d + count - slot) % count) for d in range(count)]
        slots.append(lax.ppermute(blocks_of(target), axis, pairs))
    return slots


def local_heads(patch_rows, qkv_blocks, out_blocks, out_grad):
    depth = lax.axis_size("depth")
    grid_index = lax.axis_index("grid")
    row_place, col_place = grid_index // 2, grid_index % 2
    depth_place = lax.axis_index("depth")
    table = arrivals(depth)
    offsets = [0] + [
        sum(
            jnp.where(depth_place == d, (step if side == 0 else depth - step), 0)
            for d, (side, step) in enumerate(table[d][index] for d in range(depth))
        )
        for index in range(depth - 1)
    ]
    place = jnp.stack([row_place, col_place, *offsets]).astype(jnp.int32)
    heads_local, head_dim = qkv_blocks.shape[3:]
    heads_half = heads_local // 2
    half = heads_half * head_dim
    weights = qkv_blocks[0].transpose(1, 2, 0, 3)
    w_back = out_blocks[0]
    low = jnp.bfloat16
    sizes = SIZES if heads_half == sum(SIZES) else [heads_half]
    chunks = [(sum(sizes[:index]), size) for index, size in enumerate(sizes)]

    x_other = core_swap(patch_rows)
    g_other = core_swap(out_grad)
    received = []
    for start, heads in chunks:
        send = project(place, patch_rows, x_other, weights, 1, start, heads, low)
        received.append(y_swap(send))
    g_line = ([out_grad], [out_grad])
    line_step(*g_line, "depth")
    line_step(*g_line, "depth")
    grad_panel = ordered(col_place, out_grad, g_other, 1)
    d_att_partial = contract(grad_panel, w_back, 1, 1)
    d_att_send = lax.dynamic_slice_in_dim(d_att_partial, (1 - row_place) * half, half, 1)
    d_att_keep = lax.dynamic_slice_in_dim(d_att_partial, row_place * half, half, 1)
    d_attended = (d_att_keep + y_swap(d_att_send.astype(low)).astype(jnp.float32)).astype(low)

    x_panel = ordered(col_place, patch_rows, x_other, 1)
    block_rows = x_panel.shape[1] // depth
    part_rows = block_rows // 2
    x_parts = send_slots(
        lambda target: lax.dynamic_slice_in_dim(
            x_panel, target * block_rows + col_place * part_rows, part_rows, 1
        ),
        "depth",
    )

    shape = (3, heads_local, block_rows, head_dim)
    attended, d_proj = [], []
    for (start, heads), recv in zip(chunks, received):
        keep = project(place, patch_rows, x_other, weights, 0, start, heads, jnp.float32)
        parts = attend(keep, recv, d_attended, start, heads, head_dim)
        attended.append(parts[0])
        d_proj.append(parts[1])
    attended, d_proj = jnp.concatenate(attended, axis=1), jnp.concatenate(d_proj, axis=1)

    d_proj, attended, g_line, x_parts = together(d_proj, attended, g_line, x_parts)
    upper, lower = [d_proj], [d_proj]
    own, other = [d_proj], [y_swap(jnp.concatenate([d_proj, attended], axis=1))]

    line_step(upper, lower, "depth")
    slot = pick_arrival(upper, lower, 0, table, "depth")
    x_own = jnp.concatenate(x_parts, axis=0)
    x_swapped = core_swap(x_own)
    upper, lower, slot, other, x_own, x_swapped, attended = together(
        upper, lower, slot, other, x_own, x_swapped, attended
    )
    attended_panel = ordered(row_place, attended, other[0][:, d_proj.shape[1] :], 1)
    own.append(slot)
    other.append(y_swap(slot))

    line_step(upper, lower, "depth")
    slot = pick_arrival(upper, lower, 1, table, "depth")
    input_keep, input_send = input_terms(place, own[0], other[0], weights)
    out_keep, out_send = output_terms(place, attended, other[0], w_back)
    upper, lower, slot, other, input_keep, input_send, out_keep, out_send, attended_panel = together(
        upper, lower, slot, other, input_keep, input_send, out_keep, out_send, attended_panel
    )
    own.append(slot)
    other.append(y_swap(slot))

    line_step(upper, lower, "depth")
    input_grad = (input_keep + core_swap(input_send).astype(jnp.float32)).astype(low)
    slot = pick_arrival(upper, lower, 2, table, "depth")
    attention_out = (out_keep + core_swap(out_send).astype(jnp.float32)).astype(low)
    slot, x_own, input_grad, attended_panel, g_line = together(
        slot, x_own, input_grad, attended_panel, g_line
    )
    own.append(slot)
    other.append(y_swap(slot))

    line_step(*g_line, "depth")
    grad_rows = w_back.shape[0] // depth
    a_slots = send_slots(
        lambda target: lax.dynamic_slice_in_dim(
            attended_panel, target * grad_rows, grad_rows, 1
        ),
        "depth",
    )
    filled = weight_terms(place, x_own, x_swapped, own, 0, 0, shape, None)
    other, attention_out, filled = together(other, attention_out, filled)

    filled = weight_terms(place, x_own, x_swapped, other, 1, 0, shape, filled)
    g_line, a_slots, filled = together(g_line, a_slots, filled)
    g_far = jnp.concatenate(by_offset(*g_line, "depth"), axis=0)
    g_far_other = core_swap(g_far)
    out_proj_grad = out_terms(
        place,
        jnp.concatenate(a_slots, axis=0),
        [out_grad, g_far],
        [g_other, g_far_other],
    )
    qkv_grad = filled.transpose(2, 0, 1, 3)[None]
    return (attention_out, input_grad, qkv_grad, out_proj_grad[None])


def local_any(patch_rows, qkv_blocks, out_blocks, out_grad):
    by_heads = (
        lax.axis_size("grid") == 4
        and qkv_blocks.shape[3] % 2 == 0
        and patch_rows.shape[0] == PATCHES
        and qkv_blocks.shape[1] % (2 * lax.axis_size("depth")) == 0
        and out_blocks.shape[1] % lax.axis_size("depth") == 0
        and lax.axis_size("depth") == 4
    )
    body = local_heads if by_heads else local
    return body(patch_rows, qkv_blocks, out_blocks, out_grad)


def solution(mesh):
    return jax.shard_map(
        local_any,
        mesh=mesh,
        in_specs=(
            P(("groups", "depth"), "grid"),
            P("grid", None, None, None, None),
            P("grid", None, None),
            P(("groups", "depth"), "grid"),
        ),
        out_specs=(
            P(("groups", "depth"), "grid"),
            P(("groups", "depth"), "grid"),
            P(("groups", "grid"), "depth", None, None, None),
            P(("groups", "grid"), "depth", None),
        ),
        check_vma=False,
    )
```
